512 devices in a mesh: seq: 64 (over y, z), tp: 8 (over x, core).
Axes of the slice: x: 4, y: 8, z: 8, core: 2. Of those that a mesh axis runs over, the one named last changes fastest.
Arguments:
- queries: bfloat16 [8, 8, 512, 8, 128], P(None, None, 'seq', 'tp'), may hold values from -16 to 16
- span_kv: bfloat16 [8, 8, 512, 256], P(None, None, 'seq'), may hold values from -12 to 12
- cache: bfloat16 [64, 2048, 256], P('seq', 'tp'), may hold values from -12 to 12, as said below
- prefix_len: int32 [8], replicated, may hold values from 1 to 2048, 8200 in all
- span_len: int32 [8], replicated, may hold values from 1 to 512, 2056 in all
- row_source: int32 [8, 512], replicated, may hold values from 0 to 511, each once within a row
Outputs:
- attended: bfloat16 [8, 8, 512, 8, 128], P(None, None, 'seq', 'tp')
The draws below stay inside these ranges and needn't reach their ends.
Inputs may be any that keep to these rules, and one draw needn't show every extreme that they name: `cache`: cached keys and values; positions at or past a response's prefix_len hold values that must not be read. Cached positions 0 to prefix_len - 1 of each response are valid. Span positions span_len or more of a response are padding. `row_source`: each group's row holds every number of 0 to 511 once.
All inputs are finite; a program needn't handle non-finite values.
Results may differ from the reference program's by a relative error of at most 0.0045.
Values may be sent and summed in bfloat16 or wider, within the bound.
A program may use at most 64 MiB of HBM per device.

```python
import math
import jax
import jax.numpy as jnp
import numpy as np
from jax import lax

KVH = 8
HD = 128
SPAN = 512
PREFIX = 2048
GROUP = 8
RG = 8
RESPONSES = 8
TOK_RG = 512


def draw_queries(key, part):
    shape = (KVH, RG, TOK_RG, GROUP, HD)
    return jnp.clip(jax.random.normal(jax.random.fold_in(key, 1), shape, jnp.float32), -6.0, 6.0).astype(jnp.bfloat16)


def draw_span_kv(key, part):
    shape = (KVH, RG, TOK_RG, 2 * HD)
    return jnp.clip(jax.random.normal(jax.random.fold_in(key, 2), shape, jnp.float32), -6.0, 6.0).astype(jnp.bfloat16)


def draw_cache(key, part):
    shape = (KVH * RESPONSES, PREFIX, 2 * HD)
    return jnp.clip(jax.random.normal(jax.random.fold_in(key, 3), shape, jnp.float32), -6.0, 6.0).astype(jnp.bfloat16)


def length_profile(amount, total, most, lean):
    weights = [(1 << 20) // math.isqrt(grade ** lean) + 1 for grade in range(2, amount + 1)]
    spare, given = total - most - (amount - 1), [1] * (amount - 1)
    while spare > 0:
        free = [i for i in range(amount - 1) if given[i] < most]
        pool, budget = sum([weights[i] for i in free]), spare
        for i in free:
            extra = min(most - given[i], max(1, budget * weights[i] // pool), spare)
            given[i] = given[i] + extra
            spare = spare - extra
    return np.array([most] + given)


def uneven(own_key, amount, total, limit, skew):
    if amount == 2:
        one = jax.random.randint(own_key, (), max(1, total - limit), min(limit, total - 1) + 1)
        return jnp.stack([one, total - one])
    tallies = jnp.asarray(length_profile(amount, total, limit, skew), jnp.int32)
    couples = (amount - 1) // 2
    source_of, sink = tallies[1:1 + 2 * couples:2], tallies[2:2 + 2 * couples:2]
    room = jnp.minimum(source_of - 1, limit - sink)
    shifted = jax.random.randint(jax.random.fold_in(own_key, 1), (couples,), 0, 1 << 20) % (room + 1)
    tallies = tallies.at[1:1 + 2 * couples:2].set(source_of - shifted).at[2:2 + 2 * couples:2].set(sink + shifted)
    return tallies[jax.random.permutation(jax.random.fold_in(own_key, 2), amount)]


def setup_inputs(seed: int = 0) -> dict:
    key_of = jax.random.split(jax.random.key(seed), 7)
    return {
        "queries": draw_queries(jax.random.fold_in(key_of[6], 71), 0),
        "span_kv": draw_span_kv(jax.random.fold_in(key_of[6], 71), 0),
        "cache": draw_cache(jax.random.fold_in(key_of[6], 71), 0),
        "prefix_len": uneven(key_of[3], RESPONSES, RESPONSES * PREFIX // 2 + RESPONSES, PREFIX, 0).astype(jnp.int32),
        "span_len": uneven(key_of[4], RESPONSES, RESPONSES * SPAN // 2 + RESPONSES, SPAN, 0).astype(jnp.int32),
        "row_source": jax.vmap(lambda own: jax.random.permutation(own, TOK_RG))(jax.random.split(key_of[5], RG)).reshape((RG, TOK_RG)).astype(jnp.int32),
    }


def reorder(table, source):
    gathered = [jnp.take(table[:, number], source[number], axis=1) for number in range(table.shape[1])]
    return jnp.stack(gathered, axis=1)

def attend_group(operands):
    queries, fresh_rows, stored, limits, counts = operands
    head_dim = queries.shape[-1]
    span_rows = queries.shape[1]
    prefix_rows = stored.shape[1]
    key_rows = jnp.concatenate([stored[..., :head_dim], fresh_rows[..., :head_dim]], axis=1).astype(jnp.float32)
    value_rows = jnp.concatenate([stored[..., head_dim:], fresh_rows[..., head_dim:]], axis=1).astype(jnp.float32)
    scores = jnp.einsum('rqhd,rkd->rqhk', queries.astype(jnp.float32), key_rows) * (1.0 / math.sqrt(head_dim))
    places = jnp.arange(prefix_rows + span_rows, dtype=jnp.int32)
    tokens = jnp.arange(span_rows, dtype=jnp.int32)
    in_cache = places[None, None, :] < limits[:, None, None]
    causal = places[None, :] - prefix_rows <= tokens[:, None]
    visible = jnp.where(places[None, None, :] < prefix_rows, in_cache, causal[None, :, :])
    scores = jnp.where(visible[:, :, None, :], scores, -jnp.inf)
    row_max = lax.optimization_barrier(jnp.max(scores, axis=-1))
    weights = lax.optimization_barrier(jnp.exp(scores - row_max[..., None]).astype(jnp.bfloat16))
    weight_sum = lax.optimization_barrier(jnp.sum(weights.astype(jnp.float32), axis=-1))
    mixture = jnp.einsum('rqhk,rkd->rqhd', weights.astype(jnp.float32), value_rows)
    result = mixture / weight_sum[..., None]
    live_rows = tokens[None, :] < counts[:, None]
    return jnp.where(live_rows[:, :, None, None], result, 0.0).astype(jnp.bfloat16)

def reference(queries, span_kv, cache, prefix_len, span_len, row_source):
    kv_heads, group_count, token_count, group_size, head_dim = queries.shape
    responses = token_count // SPAN
    ordered = reorder(queries, row_source)
    fresh_table = reorder(span_kv, row_source)
    group_total = kv_heads * group_count
    operands = (ordered.reshape(group_total, responses, SPAN, group_size, head_dim), fresh_table.reshape(group_total, responses, SPAN, 2 * head_dim), cache.reshape(group_total, responses, PREFIX, 2 * head_dim), jnp.tile(prefix_len.reshape(group_count, responses), (kv_heads, 1)), jnp.tile(span_len.reshape(group_count, responses), (kv_heads, 1)))
    result = lax.map(attend_group, operands)
    return result.reshape(kv_heads, group_count, token_count, group_size, head_dim)
```

```python
import functools
import math

import jax
import jax.numpy as jnp
from jax import lax
from jax.experimental import pallas as pl
from jax.experimental.pallas import tpu as pltpu
from jax.sharding import PartitionSpec as P

MESH = pl.DeviceIdType.MESH
SIDE = 8
RING = 4
ROWS = 8
HD = 128
TOK = 512
SHARD = 256
FAR_FIRST = (4, 3, 5, 2, 6, 1, 7)


def kernel(
    q_hbm,
    kv_hbm,
    cache_hbm,
    plen_hbm,
    slen_hbm,
    rs_hbm,
    out_ref,
    q_loc,
    kv_loc,
    q_mid,
    q_all,
    kv_mid,
    kv_all,
    stored,
    plen,
    slen,
    rs,
    pick,
    q_tab,
    m_tab,
    acc_tab,
    att,
    loc_sem,
    send_sem,
    recv_sem,
    ring_send,
    ring_recv,
):
    s = lax.axis_index("seq")
    t = lax.axis_index("tp")
    y, z = s // SIDE, s % SIDE
    x, core = t // 2, t % 2
    other = x * 2 + 1 - core
    right = lax.rem(x + 1, RING) * 2 + core
    left = lax.rem(x + RING - 1, RING) * 2 + core
    x_right, x_left = lax.rem(x + 1, RING), lax.rem(x + RING - 1, RING)
    x_far = lax.rem(x + 2, RING)

    def along_z(d):
        return y * SIDE + lax.rem(z + d, SIDE)

    def along_y(d):
        return lax.rem(y + d, SIDE) * SIDE + z

    barrier = pltpu.get_barrier_semaphore()
    for d in range(1, SIDE):
        pl.semaphore_signal(barrier, inc=1, device_id={"seq": along_z(d)}, device_id_type=MESH)
        pl.semaphore_signal(barrier, inc=1, device_id={"seq": along_y(d)}, device_id_type=MESH)
    for peer in (other, right, left):
        pl.semaphore_signal(barrier, inc=1, device_id={"tp": peer}, device_id_type=MESH)

    half = pl.ds(pl.multiple_of(core * HD, HD), HD)
    loads = [
        pltpu.make_async_copy(q_hbm, q_loc, loc_sem.at[0]),
        pltpu.make_async_copy(kv_hbm.at[:, :, :, half], kv_loc, loc_sem.at[1]),
        pltpu.make_async_copy(cache_hbm, stored.at[pl.ds(t, 1)], loc_sem.at[2]),
        pltpu.make_async_copy(plen_hbm, plen, loc_sem.at[3]),
        pltpu.make_async_copy(slen_hbm, slen, loc_sem.at[4]),
        pltpu.make_async_copy(rs_hbm, rs, loc_sem.at[5]),
    ]
    for load in loads:
        load.start()
    for load in loads:
        load.wait()

    pl.semaphore_wait(barrier, 2 * (SIDE - 1) + 3)

    def push(src, dst, send, recv, **where):
        copy = pltpu.make_async_remote_copy(
            src_ref=src, dst_ref=dst, send_sem=send, recv_sem=recv, device_id=where, device_id_type=MESH
        )
        copy.start()
        return copy

    for d in FAR_FIRST:
        to_z, to_y = lax.rem(z + d, SIDE), lax.rem(y + d, SIDE)
        push(q_loc.at[:, to_z], q_mid.at[z], send_sem.at[0], recv_sem.at[0], seq=along_z(d))
        push(kv_loc.at[to_y], kv_mid.at[y], send_sem.at[1], recv_sem.at[1], seq=along_y(d))
    own_q = pltpu.make_async_copy(q_loc.at[:, z], q_mid.at[z], loc_sem.at[0])
    own_kv = pltpu.make_async_copy(kv_loc.at[y], kv_mid.at[y], loc_sem.at[1])
    own_q.start()
    own_kv.start()

    mine = stored.at[t]
    ring = [
        push(mine, mine, ring_send.at[0], ring_recv.at[0], tp=right),
        push(mine, mine, ring_send.at[1], ring_recv.at[1], tp=left),
        push(mine, mine, ring_send.at[2], ring_recv.at[2], tp=other),
    ]

    source = rs[pl.ds(z, 1), :].astype(jnp.float32)
    source = jnp.broadcast_to(source, (HD, TOK)).T
    lane = lax.broadcasted_iota(jnp.int32, (TOK, HD), 1).astype(jnp.float32)
    row = lax.broadcasted_iota(jnp.int32, (TOK, HD), 0).astype(jnp.float32)
    places = []
    for block in range(TOK // HD):
        hit = source == lane + float(block * HD)
        pick[:, block * HD : (block + 1) * HD] = jnp.where(hit, 1.0, 0.0).astype(jnp.bfloat16)
        places.append(jnp.sum(jnp.where(hit, row, 0.0), axis=0, keepdims=True))
    place = jnp.concatenate(places, axis=1)

    own_q.wait()
    pltpu.make_async_copy(q_mid.at[pl.ds(0, SIDE - 1)], q_mid.at[pl.ds(0, SIDE - 1)], recv_sem.at[0]).wait()
    for d in FAR_FIRST:
        push(q_mid.at[:, lax.rem(y + d, SIDE)], q_all.at[y], send_sem.at[2], recv_sem.at[2], seq=along_y(d))
    own_q = pltpu.make_async_copy(q_mid.at[:, y], q_all.at[y], loc_sem.at[0])
    own_q.start()

    own_kv.wait()
    pltpu.make_async_copy(kv_mid.at[pl.ds(0, SIDE - 1)], kv_mid.at[pl.ds(0, SIDE - 1)], recv_sem.at[1]).wait()
    for d in FAR_FIRST:
        push(
            kv_mid.at[:, lax.rem(z + d, SIDE)], kv_all.at[core, :, z], send_sem.at[3], recv_sem.at[3], seq=along_z(d)
        )
    own_kv = pltpu.make_async_copy(kv_mid.at[:, z], kv_all.at[core, :, z], loc_sem.at[1])
    own_kv.start()

    low, high = pl.ds(0, SHARD // 2), pl.ds(SHARD // 2, SHARD // 2)
    from_left, from_right, from_far = x_left * 2 + core, x_right * 2 + core, x_far * 2 + core
    ring[0].wait_recv()
    ring.append(push(stored.at[from_left, low], stored.at[from_left, low], ring_send.at[3], ring_recv.at[3], tp=right))
    ring.append(push(stored.at[from_left], stored.at[from_left], ring_send.at[4], ring_recv.at[4], tp=other))
    ring[1].wait_recv()
    ring.append(push(stored.at[from_right, high], stored.at[from_right, high], ring_send.at[5], ring_recv.at[5], tp=left))
    ring.append(push(stored.at[from_right], stored.at[from_right], ring_send.at[6], ring_recv.at[6], tp=other))
    ring[3].wait_recv()
    ring[5].wait_recv()
    ring.append(push(stored.at[from_far], stored.at[from_far], ring_send.at[7], ring_recv.at[7], tp=other))
    for step in (2, 4, 6, 7):
        ring[step].wait_recv()

    own_q.wait()
    pltpu.make_async_copy(q_all.at[pl.ds(0, SIDE - 1)], q_all.at[pl.ds(0, SIDE - 1)], recv_sem.at[2]).wait()
    rows_q = q_all[...].reshape(TOK, HD)
    q_tab[...] = jnp.dot(pick[...], rows_q, preferred_element_type=jnp.float32).astype(jnp.bfloat16)

    rate = math.log2(math.e) / math.sqrt(HD)
    contract = (((1,), (1,)), ((), ()))
    block = 128
    keys = RING * 2 * SHARD
    limit = plen[z]

    def cache_block(number, carry):
        rows = pl.ds(pl.multiple_of(number * block, block), block)
        scores = lax.dot_general(
            q_tab[rows, :],
            stored[:, :, :HD].reshape(keys, HD),
            contract,
            preferred_element_type=jnp.float32,
        )
        seen = lax.broadcasted_iota(jnp.int32, (block, keys), 1) < limit
        scores = jnp.where(seen, scores, -jnp.inf)
        top = jnp.max(scores, axis=1, keepdims=True)
        weights = jnp.exp2((scores - top) * rate).astype(jnp.bfloat16)
        values = jnp.concatenate([stored[:, :, HD:].reshape(keys, HD), jnp.ones((keys, HD), jnp.bfloat16)], axis=1)
        acc_tab[rows, :] = jnp.dot(weights, values, preferred_element_type=jnp.float32)
        m_tab[rows, :] = jnp.broadcast_to(top, (block, HD))
        return carry

    lax.fori_loop(0, TOK // block, cache_block, 0)

    own_kv.wait()
    pltpu.make_async_copy(kv_all.at[0, pl.ds(0, SIDE - 1)], kv_all.at[0, pl.ds(0, SIDE - 1)], recv_sem.at[3]).wait()
    swap = push(kv_all.at[core], kv_all.at[core], ring_send.at[8], ring_recv.at[8], tp=other)
    swap.wait_recv()

    live = slen[z]

    def span_block(step, carry):
        number = lax.rem(y // 2 + 2 + step, TOK // block)
        start = pl.multiple_of(number * block, block)
        rows = pl.ds(start, block)
        scores = lax.dot_general(
            q_tab[rows, :], kv_all[0].reshape(TOK, HD), contract, preferred_element_type=jnp.float32
        )
        token = (lax.broadcasted_iota(jnp.int32, (block, TOK), 0) + start).astype(jnp.float32)
        scores = jnp.where(place <= token, scores, -jnp.inf)
        before = m_tab[rows, :][:, :1]
        top = jnp.maximum(before, jnp.max(scores, axis=1, keepdims=True))
        weights = jnp.exp2((scores - top) * rate).astype(jnp.bfloat16)
        values = jnp.concatenate([kv_all[1].reshape(TOK, HD), jnp.ones((TOK, HD), jnp.bfloat16)], axis=1)
        total = acc_tab[rows, :] * jnp.exp2((before - top) * rate)
        total = total + jnp.dot(weights, values, preferred_element_type=jnp.float32)
        result = total[:, :HD] / total[:, HD:]
        token = lax.broadcasted_iota(jnp.int32, (block, HD), 0) + start
        result = jnp.where(token < live, result, 0.0).astype(jnp.bfloat16)
        att[pl.ds(number * (block // ROWS), block // ROWS)] = result.reshape(block // ROWS, ROWS, HD)
        return carry

    def send_block(step, carry):
        number = lax.rem(y // 2 + 2 + step, TOK // block)

        def send_one(i, carry):
            to = number * (block // ROWS) + i

            @pl.when(to != s)
            def _():
                push(att.at[to], out_ref.at[s], send_sem.at[4], recv_sem.at[4], seq=to)

            return carry

        return lax.fori_loop(0, block // ROWS, send_one, carry)

    def both(step, carry):
        span_block(step, carry)
        return send_block(step, carry)

    lax.fori_loop(0, TOK // block, both, 0)
    own = pltpu.make_async_copy(att.at[s], out_ref.at[s], loc_sem.at[0])
    own.start()

    for step in range(8):
        ring[step].wait_send()
    swap.wait_send()
    for stage in range(4):
        pltpu.make_async_copy(q_all.at[pl.ds(0, SIDE - 1)], q_all.at[pl.ds(0, SIDE - 1)], send_sem.at[stage]).wait()
    own.wait()
    peers = SIDE * SIDE - 1
    pltpu.make_async_copy(att.at[pl.ds(0, peers)], att.at[pl.ds(0, peers)], send_sem.at[4]).wait()
    pltpu.make_async_copy(out_ref.at[pl.ds(0, peers)], out_ref.at[pl.ds(0, peers)], recv_sem.at[4]).wait()


def on_device(queries, span_kv, cache, prefix_len, span_len, row_source):
    shape = queries.shape
    hbm = pl.BlockSpec(memory_space=pl.ANY)
    tile = (SIDE, SIDE, ROWS, HD)
    out = pl.pallas_call(
        kernel,
        out_shape=jax.ShapeDtypeStruct((SIDE * SIDE, ROWS, HD), jnp.bfloat16),
        in_specs=[hbm] * 6,
        out_specs=hbm,
        scratch_shapes=[
            pltpu.VMEM(tile, jnp.bfloat16),
            pltpu.VMEM(tile, jnp.bfloat16),
            pltpu.VMEM(tile, jnp.bfloat16),
            pltpu.VMEM(tile, jnp.bfloat16),
            pltpu.VMEM(tile, jnp.bfloat16),
            pltpu.VMEM((2,) + tile, jnp.bfloat16),
            pltpu.VMEM((RING * 2, SHARD, 2 * HD), jnp.bfloat16),
            pltpu.SMEM((8,), jnp.int32),
            pltpu.SMEM((8,), jnp.int32),
            pltpu.VMEM((8, TOK), jnp.int32),
            pltpu.VMEM((TOK, TOK), jnp.bfloat16),
            pltpu.VMEM((TOK, HD), jnp.bfloat16),
            pltpu.VMEM((TOK, HD), jnp.float32),
            pltpu.VMEM((TOK, 2 * HD), jnp.float32),
            pltpu.VMEM((SIDE * SIDE, ROWS, HD), jnp.bfloat16),
            pltpu.SemaphoreType.DMA((6,)),
            pltpu.SemaphoreType.DMA((5,)),
            pltpu.SemaphoreType.DMA((5,)),
            pltpu.SemaphoreType.DMA((9,)),
            pltpu.SemaphoreType.DMA((9,)),
        ],
        compiler_params=pltpu.CompilerParams(collective_id=0, has_side_effects=True),
    )(
        queries.reshape(tile),
        span_kv,
        cache,
        prefix_len,
        span_len,
        row_source,
    )
    return out.reshape(shape)


def solution(mesh):
    in_specs = (
        P(None, None, "seq", "tp", None),
        P(None, None, "seq", None),
        P("seq", "tp", None),
        P(),
        P(),
        P(),
    )
    out_specs = P(None, None, "seq", "tp", None)
    return jax.shard_map(on_device, mesh=mesh, in_specs=in_specs, out_specs=out_specs, check_vma=False)
```

```python
import functools
import math

import jax
import jax.numpy as jnp
from jax import lax
from jax.experimental import pallas as pl
from jax.experimental.pallas import tpu as pltpu
from jax.sharding import PartitionSpec as P

MESH = pl.DeviceIdType.MESH
SIDE = 8
RING = 4
ROWS = 8
HD = 128
TOK = 512
SHARD = 256
GROUP = 64
FAR_FIRST = (4, 3, 5, 2, 6, 1, 7)
SEND_ORDER = FAR_FIRST + (0,)


def kernel(
    q_hbm,
    kv_hbm,
    cache_hbm,
    plen_hbm,
    slen_hbm,
    rs_hbm,
    out_ref,
    q_mid,
    q_all,
    kv_mid,
    kv_all,
    stored,
    plen,
    slen,
    rs,
    source_tab,
    pick,
    q_tab,
    att,
    loc_sem,
    send_sem,
    recv_sem,
    ring_send,
    ring_recv,
):
    s = lax.axis_index("seq")
    t = lax.axis_index("tp")
    y, z = s // SIDE, s % SIDE
    x, core = t // 2, t % 2
    other = x * 2 + 1 - core
    x_right, x_left, x_far = lax.rem(x + 1, RING), lax.rem(x + RING - 1, RING), lax.rem(x + 2, RING)
    right, left, far = x_right * 2 + core, x_left * 2 + core, x_far * 2 + core
    ys = [lax.rem(y + d, SIDE) for d in range(SIDE)]
    zs = [lax.rem(z + d, SIDE) for d in range(SIDE)]

    barrier = pltpu.get_barrier_semaphore()
    for d in FAR_FIRST:
        pl.semaphore_signal(barrier, inc=1, device_id={"seq": y * SIDE + zs[d]}, device_id_type=MESH)
        pl.semaphore_signal(barrier, inc=1, device_id={"seq": ys[d] * SIDE + z}, device_id_type=MESH)
    for peer in (other, right, left):
        pl.semaphore_signal(barrier, inc=1, device_id={"tp": peer}, device_id_type=MESH)
    with jax.named_scope("W_barrier"):
        pl.semaphore_wait(barrier, 2 * (SIDE - 1) + 3)

    def push(src, dst, send, recv, **where):
        copy = pltpu.make_async_remote_copy(
            src_ref=src, dst_ref=dst, send_sem=send, recv_sem=recv, device_id=where, device_id_type=MESH
        )
        copy.start()
        return copy

    def take(src, dst, sem):
        copy = pltpu.make_async_copy(src, dst, sem)
        copy.start()
        return copy

    def await_all(ref, sem):
        pltpu.make_async_copy(ref, ref, sem).wait()

    half = pl.ds(pl.multiple_of(core * HD, HD), HD)
    for d in FAR_FIRST:
        push(q_hbm.at[:, zs[d]], q_mid.at[z], send_sem.at[0], recv_sem.at[0], seq=y * SIDE + zs[d])
        push(kv_hbm.at[ys[d], :, :, half], kv_mid.at[y], send_sem.at[1], recv_sem.at[1], seq=ys[d] * SIDE + z)
    own_q = take(q_hbm.at[:, z], q_mid.at[z], loc_sem.at[0])
    own_kv = take(kv_hbm.at[y, :, :, half], kv_mid.at[y], loc_sem.at[1])

    shard = cache_hbm.at[0]
    ring = [
        push(shard, stored.at[t], ring_send.at[0], ring_recv.at[0], tp=right),
        push(shard, stored.at[t], ring_send.at[1], ring_recv.at[1], tp=left),
        push(shard, stored.at[t], ring_send.at[2], ring_recv.at[2], tp=other),
    ]
    own_shard = take(shard, stored.at[t], loc_sem.at[2])
    small = [
        take(plen_hbm, plen, loc_sem.at[3]),
        take(slen_hbm, slen, loc_sem.at[4]),
        take(rs_hbm, rs, loc_sem.at[5]),
    ]
    for load in small:
        load.wait()

    source = rs[pl.ds(z, 1), :].astype(jnp.float32)
    source = jnp.broadcast_to(source, (HD, TOK)).T
    source_tab[...] = source
    row = lax.broadcasted_iota(jnp.int32, (TOK, HD), 0).astype(jnp.float32)
    lane = lax.broadcasted_iota(jnp.int32, (TOK, HD), 1).astype(jnp.float32)
    places = [
        jnp.sum(jnp.where(source == lane + float(part * HD), row, 0.0), axis=0, keepdims=True)
        for part in range(TOK // HD)
    ]
    place = jnp.concatenate(places, axis=1)
    lane = lax.broadcasted_iota(jnp.int32, (GROUP, HD), 1).astype(jnp.float32)
    for number, d in enumerate(SEND_ORDER):
        source = source_tab[pl.ds(pl.multiple_of(ys[d] * GROUP, GROUP), GROUP), :]
        for part in range(TOK // HD):
            pick[number * GROUP : (number + 1) * GROUP, part * HD : (part + 1) * HD] = jnp.where(
                source == lane + float(part * HD), 1.0, 0.0
            ).astype(jnp.bfloat16)

    with jax.named_scope("W_q1"):
        own_q.wait()
        await_all(q_mid.at[pl.ds(0, SIDE - 1)], recv_sem.at[0])
    for d in FAR_FIRST:
        push(q_mid.at[:, ys[d]], q_all.at[y], send_sem.at[2], recv_sem.at[2], seq=ys[d] * SIDE + z)
    own_q = take(q_mid.at[:, y], q_all.at[y], loc_sem.at[0])

    with jax.named_scope("W_kv1"):
        own_kv.wait()
        await_all(kv_mid.at[pl.ds(0, SIDE - 1)], recv_sem.at[1])
    for d in FAR_FIRST:
        push(kv_mid.at[:, zs[d]], kv_all.at[core, :, z], send_sem.at[3], recv_sem.at[3], seq=y * SIDE + zs[d])
    own_kv = take(kv_mid.at[:, z], kv_all.at[core, :, z], loc_sem.at[1])

    low, high = pl.ds(0, SHARD // 2), pl.ds(SHARD // 2, SHARD // 2)
    with jax.named_scope("W_ring01"):
        ring[0].wait_recv()
        ring[1].wait_recv()
    ring.append(push(stored.at[left, low], stored.at[left, low], ring_send.at[3], ring_recv.at[3], tp=right))
    ring.append(push(stored.at[right, high], stored.at[right, high], ring_send.at[4], ring_recv.at[4], tp=left))
    ring.append(push(stored.at[left], stored.at[left], ring_send.at[5], ring_recv.at[5], tp=other))
    ring.append(push(stored.at[right], stored.at[right], ring_send.at[6], ring_recv.at[6], tp=other))
    with jax.named_scope("W_ring34"):
        ring[3].wait_recv()
        ring[4].wait_recv()
    ring.append(push(stored.at[far], stored.at[far], ring_send.at[7], ring_recv.at[7], tp=other))

    with jax.named_scope("W_kv2"):
        own_kv.wait()
        await_all(kv_all.at[0, pl.ds(0, SIDE - 1)], recv_sem.at[3])
    swap = push(kv_all.at[core], kv_all.at[core], ring_send.at[8], ring_recv.at[8], tp=other)

    with jax.named_scope("W_q2"):
        own_q.wait()
        await_all(q_all.at[pl.ds(0, SIDE - 1)], recv_sem.at[2])
    with jax.named_scope("C_perm"):
        q_tab[...] = jnp.dot(
            pick[...], q_all[...].reshape(TOK, HD), preferred_element_type=jnp.float32
        ).astype(jnp.bfloat16)
    with jax.named_scope("W_ringall"):
        own_shard.wait()
        for step in (2, 5, 6, 7):
            ring[step].wait_recv()

    rate = math.log2(math.e) / math.sqrt(HD)
    contract = (((1,), (1,)), ((), ()))
    block = 2 * GROUP
    keys = RING * 2 * SHARD
    limit = plen[z]
    live = slen[z]

    def cache_scores(number):
        rows = q_tab[number * block : (number + 1) * block, :]
        scores = lax.dot_general(
            rows, stored[:, :, :HD].reshape(keys, HD), contract, preferred_element_type=jnp.float32
        )
        seen = lax.broadcasted_iota(jnp.int32, (block, keys), 1) < limit
        return jnp.where(seen, scores, -jnp.inf)

    def tokens(number, width):
        first, second = SEND_ORDER[2 * number], SEND_ORDER[2 * number + 1]
        counted = lax.broadcasted_iota(jnp.int32, (GROUP, width), 0)
        return jnp.concatenate([counted + ys[first] * GROUP, counted + ys[second] * GROUP], axis=0)

    def span_scores(number):
        rows = q_tab[number * block : (number + 1) * block, :]
        scores = lax.dot_general(
            rows, kv_all[0].reshape(TOK, HD), contract, preferred_element_type=jnp.float32
        )
        return jnp.where(place <= tokens(number, TOK).astype(jnp.float32), scores, -jnp.inf)

    def attend(number, held, fresh):
        top = jnp.maximum(jnp.max(held, axis=1, keepdims=True), jnp.max(fresh, axis=1, keepdims=True))
        held = jnp.exp2((held - top) * rate).astype(jnp.bfloat16)
        fresh = jnp.exp2((fresh - top) * rate).astype(jnp.bfloat16)
        values = jnp.concatenate([stored[:, :, HD:].reshape(keys, HD), jnp.ones((keys, HD), jnp.bfloat16)], axis=1)
        total = jnp.dot(held, values, preferred_element_type=jnp.float32)
        values = jnp.concatenate([kv_all[1].reshape(TOK, HD), jnp.ones((TOK, HD), jnp.bfloat16)], axis=1)
        total = total + jnp.dot(fresh, values, preferred_element_type=jnp.float32)
        result = total[:, :HD] / total[:, HD:]
        result = jnp.where(tokens(number, HD) < live, result, 0.0).astype(jnp.bfloat16)
        att[2 * number : 2 * number + 2] = result.reshape(2, SIDE, ROWS, HD)
        for piece in (2 * number, 2 * number + 1):
            d = SEND_ORDER[piece]
            for e in SEND_ORDER:
                if d or e:
                    push(
                        att.at[piece, zs[e]],
                        out_ref.at[s],
                        send_sem.at[4],
                        recv_sem.at[4],
                        seq=ys[d] * SIDE + zs[e],
                    )

    with jax.named_scope("C_cache0"):
        held = cache_scores(0)
    with jax.named_scope("W_swap"):
        swap.wait_recv()
    fresh = span_scores(0)
    for number in range(TOK // block):
        with jax.named_scope(f"C_block{number}"):
            last = number == TOK // block - 1
            following = None if last else (cache_scores(number + 1), span_scores(number + 1))
            attend(number, held, fresh)
            if not last:
                held, fresh = following
    own = take(att.at[SIDE - 1, z], out_ref.at[s], loc_sem.at[0])

    for step in range(8):
        ring[step].wait_send()
    swap.wait_send()
    for stage in range(4):
        await_all(q_all.at[pl.ds(0, SIDE - 1)], send_sem.at[stage])
    own.wait()
    peers = pl.ds(0, SIDE * SIDE - 1)
    with jax.named_scope("W_outsend"):
        await_all(out_ref.at[peers], send_sem.at[4])
    with jax.named_scope("W_out"):
        await_all(out_ref.at[peers], recv_sem.at[4])


def on_device(queries, span_kv, cache, prefix_len, span_len, row_source):
    shape = queries.shape
    hbm = pl.BlockSpec(memory_space=pl.ANY)
    tile = (SIDE, SIDE, ROWS, HD)
    out = pl.pallas_call(
        kernel,
        out_shape=jax.ShapeDtypeStruct((SIDE * SIDE, ROWS, HD), jnp.bfloat16),
        in_specs=[hbm] * 6,
        out_specs=pl.BlockSpec(memory_space=pltpu.VMEM),
        scratch_shapes=[
            pltpu.VMEM(tile, jnp.bfloat16),
            pltpu.VMEM(tile, jnp.bfloat16),
            pltpu.VMEM(tile, jnp.bfloat16),
            pltpu.VMEM((2,) + tile, jnp.bfloat16),
            pltpu.VMEM((RING * 2, SHARD, 2 * HD), jnp.bfloat16),
            pltpu.SMEM((8,), jnp.int32),
            pltpu.SMEM((8,), jnp.int32),
            pltpu.VMEM((8, TOK), jnp.int32),
            pltpu.VMEM((TOK, HD), jnp.float32),
            pltpu.VMEM((TOK, TOK), jnp.bfloat16),
            pltpu.VMEM((TOK, HD), jnp.bfloat16),
            pltpu.VMEM(tile, jnp.bfloat16),
            pltpu.SemaphoreType.DMA((6,)),
            pltpu.SemaphoreType.DMA((5,)),
            pltpu.SemaphoreType.DMA((5,)),
            pltpu.SemaphoreType.DMA((9,)),
            pltpu.SemaphoreType.DMA((9,)),
        ],
        compiler_params=pltpu.CompilerParams(collective_id=0, has_side_effects=True),
    )(
        queries.reshape(tile),
        span_kv,
        cache,
        prefix_len,
        span_len,
        row_source,
    )
    return out.reshape(shape)


def solution(mesh):
    in_specs = (
        P(None, None, "seq", "tp", None),
        P(None, None, "seq", None),
        P("seq", "tp", None),
        P(),
        P(),
        P(),
    )
    out_specs = P(None, None, "seq", "tp", None)
    return jax.shard_map(on_device, mesh=mesh, in_specs=in_specs, out_specs=out_specs, check_vma=False)
```

```python
import functools
import math

import jax
import jax.numpy as jnp
from jax import lax
from jax.experimental import pallas as pl
from jax.experimental.pallas import tpu as pltpu
from jax.sharding import PartitionSpec as P

MESH = pl.DeviceIdType.MESH
SIDE = 8
RING = 4
ROWS = 8
HD = 128
TOK = 512
SHARD = 256
GROUP = 64
FAR_FIRST = (4, 3, 5, 2, 6, 1, 7)
SEND_ORDER = FAR_FIRST + (0,)


def kernel(
    q_hbm,
    kv_hbm,
    cache_hbm,
    plen_hbm,
    slen_hbm,
    rs_hbm,
    out_ref,
    q_mid,
    q_all,
    kv_mid,
    kv_all,
    stored,
    plen,
    slen,
    rs,
    source_tab,
    pick,
    q_tab,
    att,
    loc_sem,
    send_sem,
    recv_sem,
    ring_send,
    ring_recv,
):
    s = lax.axis_index("seq")
    t = lax.axis_index("tp")
    y, z = s // SIDE, s % SIDE
    x, core = t // 2, t % 2
    other = x * 2 + 1 - core
    x_right, x_left, x_far = lax.rem(x + 1, RING), lax.rem(x + RING - 1, RING), lax.rem(x + 2, RING)
    right, left, far = x_right * 2 + core, x_left * 2 + core, x_far * 2 + core
    ys = [lax.rem(y + d, SIDE) for d in range(SIDE)]
    zs = [lax.rem(z + d, SIDE) for d in range(SIDE)]

    barrier = pltpu.get_barrier_semaphore()
    for d in FAR_FIRST:
        pl.semaphore_signal(barrier, inc=1, device_id={"seq": y * SIDE + zs[d]}, device_id_type=MESH)
        pl.semaphore_signal(barrier, inc=1, device_id={"seq": ys[d] * SIDE + z}, device_id_type=MESH)
    for peer in (other, right, left):
        pl.semaphore_signal(barrier, inc=1, device_id={"tp": peer}, device_id_type=MESH)
    with jax.named_scope("W_barrier"):
        pl.semaphore_wait(barrier, 2 * (SIDE - 1) + 3)

    def push(src, dst, send, recv, **where):
        copy = pltpu.make_async_remote_copy(
            src_ref=src, dst_ref=dst, send_sem=send, recv_sem=recv, device_id=where, device_id_type=MESH
        )
        copy.start()
        return copy

    def take(src, dst, sem):
        copy = pltpu.make_async_copy(src, dst, sem)
        copy.start()
        return copy

    def await_all(ref, sem):
        pltpu.make_async_copy(ref, ref, sem).wait()

    half = pl.ds(pl.multiple_of(core * HD, HD), HD)
    for d in FAR_FIRST:
        push(q_hbm.at[:, zs[d]], q_mid.at[z], send_sem.at[0], recv_sem.at[0], seq=y * SIDE + zs[d])
        push(kv_hbm.at[ys[d], :, :, half], kv_mid.at[y], send_sem.at[1], recv_sem.at[1], seq=ys[d] * SIDE + z)
    own_q = take(q_hbm.at[:, z], q_mid.at[z], loc_sem.at[0])
    own_kv = take(kv_hbm.at[y, :, :, half], kv_mid.at[y], loc_sem.at[1])

    shard = cache_hbm.at[0]
    ring = [
        push(shard, stored.at[t], ring_send.at[0], ring_recv.at[0], tp=right),
        push(shard, stored.at[t], ring_send.at[1], ring_recv.at[1], tp=left),
        push(shard, stored.at[t], ring_send.at[2], ring_recv.at[2], tp=other),
    ]
    own_shard = take(shard, stored.at[t], loc_sem.at[2])
    small = [
        take(plen_hbm, plen, loc_sem.at[3]),
        take(slen_hbm, slen, loc_sem.at[4]),
        take(rs_hbm, rs, loc_sem.at[5]),
    ]
    for load in small:
        load.wait()

    source = rs[pl.ds(z, 1), :].astype(jnp.float32)
    source = jnp.broadcast_to(source, (HD, TOK)).T
    source_tab[...] = source
    row = lax.broadcasted_iota(jnp.int32, (TOK, HD), 0).astype(jnp.float32)
    lane = lax.broadcasted_iota(jnp.int32, (TOK, HD), 1).astype(jnp.float32)
    places = [
        jnp.sum(jnp.where(source == lane + float(part * HD), row, 0.0), axis=0, keepdims=True)
        for part in range(TOK // HD)
    ]
    place = jnp.concatenate(places, axis=1)
    lane = lax.broadcasted_iota(jnp.int32, (GROUP, HD), 1).astype(jnp.float32)
    for number, d in enumerate(SEND_ORDER):
        source = source_tab[pl.ds(pl.multiple_of(ys[d] * GROUP, GROUP), GROUP), :]
        for part in range(TOK // HD):
            pick[number * GROUP : (number + 1) * GROUP, part * HD : (part + 1) * HD] = jnp.where(
                source == lane + float(part * HD), 1.0, 0.0
            ).astype(jnp.bfloat16)

    low, high = pl.ds(0, SHARD // 2), pl.ds(SHARD // 2, SHARD // 2)
    with jax.named_scope("W_ring01"):
        ring[0].wait_recv()
        ring[1].wait_recv()
    ring.append(push(stored.at[left, low], stored.at[left, low], ring_send.at[3], ring_recv.at[3], tp=right))
    ring.append(push(stored.at[right, high], stored.at[right, high], ring_send.at[4], ring_recv.at[4], tp=left))
    ring.append(push(stored.at[left], stored.at[left], ring_send.at[5], ring_recv.at[5], tp=other))
    ring.append(push(stored.at[right], stored.at[right], ring_send.at[6], ring_recv.at[6], tp=other))

    with jax.named_scope("W_q1"):
        own_q.wait()
        await_all(q_mid.at[pl.ds(0, SIDE - 1)], recv_sem.at[0])
    for d in FAR_FIRST:
        push(q_mid.at[:, ys[d]], q_all.at[y], send_sem.at[2], recv_sem.at[2], seq=ys[d] * SIDE + z)
    own_q = take(q_mid.at[:, y], q_all.at[y], loc_sem.at[0])

    with jax.named_scope("W_kv1"):
        own_kv.wait()
        await_all(kv_mid.at[pl.ds(0, SIDE - 1)], recv_sem.at[1])
    for d in FAR_FIRST:
        push(kv_mid.at[:, zs[d]], kv_all.at[core, :, z], send_sem.at[3], recv_sem.at[3], seq=y * SIDE + zs[d])
    own_kv = take(kv_mid.at[:, z], kv_all.at[core, :, z], loc_sem.at[1])

    with jax.named_scope("W_ring34"):
        ring[3].wait_recv()
        ring[4].wait_recv()
    ring.append(push(stored.at[far], stored.at[far], ring_send.at[7], ring_recv.at[7], tp=other))

    with jax.named_scope("W_kv2"):
        own_kv.wait()
        await_all(kv_all.at[0, pl.ds(0, SIDE - 1)], recv_sem.at[3])
    swap = push(kv_all.at[core], kv_all.at[core], ring_send.at[8], ring_recv.at[8], tp=other)

    with jax.named_scope("W_q2"):
        own_q.wait()
        await_all(q_all.at[pl.ds(0, SIDE - 1)], recv_sem.at[2])
    with jax.named_scope("W_ringall"):
        own_shard.wait()
        for step in (2, 5, 6, 7):
            ring[step].wait_recv()

    rate = math.log2(math.e) / math.sqrt(HD)
    contract = (((1,), (1,)), ((), ()))
    block = 2 * GROUP
    keys = RING * 2 * SHARD
    limit = plen[z]
    live = slen[z]

    def cache_scores(number):
        rows = slice(number * block, (number + 1) * block)
        rows_q = jnp.dot(pick[rows, :], q_all[...].reshape(TOK, HD), preferred_element_type=jnp.float32)
        rows_q = rows_q.astype(jnp.bfloat16)
        q_tab[rows, :] = rows_q
        scores = lax.dot_general(
            rows_q, stored[:, :, :HD].reshape(keys, HD), contract, preferred_element_type=jnp.float32
        )
        seen = lax.broadcasted_iota(jnp.int32, (block, keys), 1) < limit
        return jnp.where(seen, scores, -jnp.inf)

    def tokens(number, width):
        first, second = SEND_ORDER[2 * number], SEND_ORDER[2 * number + 1]
        counted = lax.broadcasted_iota(jnp.int32, (GROUP, width), 0)
        return jnp.concatenate([counted + ys[first] * GROUP, counted + ys[second] * GROUP], axis=0)

    def span_scores(number):
        rows = q_tab[number * block : (number + 1) * block, :]
        scores = lax.dot_general(
            rows, kv_all[0].reshape(TOK, HD), contract, preferred_element_type=jnp.float32
        )
        return jnp.where(place <= tokens(number, TOK).astype(jnp.float32), scores, -jnp.inf)

    def attend(number, held, fresh):
        top = jnp.maximum(jnp.max(held, axis=1, keepdims=True), jnp.max(fresh, axis=1, keepdims=True))
        held = jnp.exp2((held - top) * rate).astype(jnp.bfloat16)
        fresh = jnp.exp2((fresh - top) * rate).astype(jnp.bfloat16)
        values = jnp.concatenate([stored[:, :, HD:].reshape(keys, HD), jnp.ones((keys, HD), jnp.bfloat16)], axis=1)
        total = jnp.dot(held, values, preferred_element_type=jnp.float32)
        values = jnp.concatenate([kv_all[1].reshape(TOK, HD), jnp.ones((TOK, HD), jnp.bfloat16)], axis=1)
        total = total + jnp.dot(fresh, values, preferred_element_type=jnp.float32)
        result = total[:, :HD] / total[:, HD:]
        result = jnp.where(tokens(number, HD) < live, result, 0.0).astype(jnp.bfloat16)
        att[2 * number : 2 * number + 2] = result.reshape(2, SIDE, ROWS, HD)
        for piece in (2 * number, 2 * number + 1):
            d = SEND_ORDER[piece]
            for e in SEND_ORDER:
                if d or e:
                    push(
                        att.at[piece, zs[e]],
                        out_ref.at[s],
                        send_sem.at[4],
                        recv_sem.at[4],
                        seq=ys[d] * SIDE + zs[e],
                    )

    with jax.named_scope("C_cache0"):
        held = cache_scores(0)
    with jax.named_scope("W_swap"):
        swap.wait_recv()
    fresh = span_scores(0)
    for number in range(TOK // block):
        with jax.named_scope(f"C_block{number}"):
            last = number == TOK // block - 1
            following = None if last else (cache_scores(number + 1), span_scores(number + 1))
            attend(number, held, fresh)
            if not last:
                held, fresh = following
    own = take(att.at[SIDE - 1, z], out_ref.at[s], loc_sem.at[0])

    for step in range(8):
        ring[step].wait_send()
    swap.wait_send()
    for stage in range(4):
        await_all(q_all.at[pl.ds(0, SIDE - 1)], send_sem.at[stage])
    own.wait()
    peers = pl.ds(0, SIDE * SIDE - 1)
    with jax.named_scope("W_outsend"):
        await_all(out_ref.at[peers], send_sem.at[4])
    with jax.named_scope("W_out"):
        await_all(out_ref.at[peers], recv_sem.at[4])


def on_device(queries, span_kv, cache, prefix_len, span_len, row_source):
    shape = queries.shape
    hbm = pl.BlockSpec(memory_space=pl.ANY)
    tile = (SIDE, SIDE, ROWS, HD)
    out = pl.pallas_call(
        kernel,
        out_shape=pltpu.VMEM((SIDE * SIDE, ROWS, HD), jnp.bfloat16),
        in_specs=[hbm] * 6,
        out_specs=pl.BlockSpec(memory_space=pltpu.VMEM),
        scratch_shapes=[
            pltpu.VMEM(tile, jnp.bfloat16),
            pltpu.VMEM(tile, jnp.bfloat16),
            pltpu.VMEM(tile, jnp.bfloat16),
            pltpu.VMEM((2,) + tile, jnp.bfloat16),
            pltpu.VMEM((RING * 2, SHARD, 2 * HD), jnp.bfloat16),
            pltpu.SMEM((8,), jnp.int32),
            pltpu.SMEM((8,), jnp.int32),
            pltpu.VMEM((8, TOK), jnp.int32),
            pltpu.VMEM((TOK, HD), jnp.float32),
            pltpu.VMEM((TOK, TOK), jnp.bfloat16),
            pltpu.VMEM((TOK, HD), jnp.bfloat16),
            pltpu.VMEM(tile, jnp.bfloat16),
            pltpu.SemaphoreType.DMA((6,)),
            pltpu.SemaphoreType.DMA((5,)),
            pltpu.SemaphoreType.DMA((5,)),
            pltpu.SemaphoreType.DMA((9,)),
            pltpu.SemaphoreType.DMA((9,)),
        ],
        compiler_params=pltpu.CompilerParams(collective_id=0, has_side_effects=True),
    )(
        queries.reshape(tile),
        span_kv,
        cache,
        prefix_len,
        span_len,
        row_source,
    )
    return out.reshape(shape)


def solution(mesh):
    in_specs = (
        P(None, None, "seq", "tp", None),
        P(None, None, "seq", None),
        P("seq", "tp", None),
        P(),
        P(),
        P(),
    )
    out_specs = P(None, None, "seq", "tp", None)
    return jax.shard_map(on_device, mesh=mesh, in_specs=in_specs, out_specs=out_specs, check_vma=False)
```

```python
import functools
import math

import jax
import jax.numpy as jnp
from jax import lax
from jax.experimental import pallas as pl
from jax.experimental.pallas import tpu as pltpu
from jax.sharding import PartitionSpec as P

MESH = pl.DeviceIdType.MESH
SIDE = 8
RING = 4
ROWS = 8
HD = 128
TOK = 512
SHARD = 256
GROUP = 64
FAR_FIRST = (4, 3, 5, 2, 6, 1, 7)
Y_ORDER = (0, 1, 2, 3, 7, 6, 5, 4)


def kernel(
    q_hbm,
    kv_hbm,
    cache_hbm,
    plen_hbm,
    slen_hbm,
    rs_hbm,
    out_ref,
    q_mid,
    q_all,
    kv_mid,
    kv_all,
    stored,
    plen,
    slen,
    rs,
    pick,
    q_tab,
    att,
    known_y,
    known_z,
    loc_sem,
    send_sem,
    recv_sem,
    piece_sem,
    ring_send,
    ring_recv,
):
    s = lax.axis_index("seq")
    t = lax.axis_index("tp")
    y, z = s // SIDE, s % SIDE
    x, core = t // 2, t % 2
    other = x * 2 + 1 - core
    x_right, x_left, x_far = lax.rem(x + 1, RING), lax.rem(x + RING - 1, RING), lax.rem(x + 2, RING)
    right, left, far = x_right * 2 + core, x_left * 2 + core, x_far * 2 + core
    ys = [lax.rem(y + d, SIDE) for d in range(SIDE)]
    zs = [lax.rem(z + d, SIDE) for d in range(SIDE)]

    rank = jnp.where(y < SIDE // 2, y, SIDE + SIDE // 2 - 1 - y)

    def signal(semaphore, **where):
        pl.semaphore_signal(semaphore, inc=1, device_id=where, device_id_type=MESH)

    barrier = pltpu.get_barrier_semaphore()
    for peer in (other, right, left):
        signal(barrier, tp=peer)
    for step in range(1, SIDE):
        pl.when(step > z)(functools.partial(signal, barrier, seq=y * SIDE + step))
        pl.when(step > rank)(functools.partial(signal, barrier, seq=Y_ORDER[step] * SIDE + z))
    with jax.named_scope("W_barrier"):
        pl.semaphore_wait(barrier, z + rank + 3)
    for step in range(SIDE - 1):
        pl.when(step < z)(functools.partial(signal, known_z.at[z], seq=y * SIDE + step))
        pl.when(step < rank)(functools.partial(signal, known_y.at[rank], seq=Y_ORDER[step] * SIDE + z))

    def push(src, dst, send, recv, **where):
        copy = pltpu.make_async_remote_copy(
            src_ref=src, dst_ref=dst, send_sem=send, recv_sem=recv, device_id=where, device_id_type=MESH
        )
        copy.start()
        return copy

    def take(src, dst, sem):
        copy = pltpu.make_async_copy(src, dst, sem)
        copy.start()
        return copy

    def await_all(ref, sem):
        pltpu.make_async_copy(ref, ref, sem).wait()

    mover = core == 1

    def send_q(to):
        push(q_hbm.at[:, to], q_mid.at[z], send_sem.at[0], recv_sem.at[0], seq=y * SIDE + to)

    def send_kv(to):
        push(kv_hbm.at[to], kv_mid.at[y], send_sem.at[1], recv_sem.at[1], seq=to * SIDE + z)

    def send_q_known(to):
        pl.semaphore_wait(known_z.at[to], 1)
        send_q(to)

    def send_kv_known(step):
        pl.semaphore_wait(known_y.at[step], 1)
        send_kv(Y_ORDER[step])

    for step in range(SIDE - 1):
        pl.when(step < z)(functools.partial(send_q, step))
        pl.when(jnp.logical_and(step < rank, mover))(functools.partial(send_kv, Y_ORDER[step]))
    own_q = take(q_hbm.at[:, z], q_mid.at[z], loc_sem.at[0])
    own_kv = pltpu.make_async_copy(kv_hbm.at[y], kv_mid.at[y], loc_sem.at[1])
    pl.when(mover)(own_kv.start)

    shard = cache_hbm.at[0]
    ring = [
        push(shard, stored.at[t], ring_send.at[0], ring_recv.at[0], tp=right),
        push(shard, stored.at[t], ring_send.at[1], ring_recv.at[1], tp=left),
        push(shard, stored.at[t], ring_send.at[2], ring_recv.at[2], tp=other),
    ]
    own_shard = take(shard, stored.at[t], loc_sem.at[2])
    small = [
        take(plen_hbm, plen, loc_sem.at[3]),
        take(slen_hbm, slen, loc_sem.at[4]),
        take(rs_hbm, rs, loc_sem.at[5]),
    ]
    for load in small:
        load.wait()

    source = rs[pl.ds(z, 1), :].astype(jnp.float32)
    source = jnp.broadcast_to(source, (HD, TOK)).T
    row = lax.broadcasted_iota(jnp.int32, (TOK, HD), 0).astype(jnp.float32)
    lane = lax.broadcasted_iota(jnp.int32, (TOK, HD), 1).astype(jnp.float32)
    places = [
        jnp.sum(jnp.where(source == lane + float(part * HD), row, 0.0), axis=0, keepdims=True)
        for part in range(TOK // HD)
    ]
    place = jnp.concatenate(places, axis=1)
    source = jnp.swapaxes(source.reshape(SIDE, SIDE, ROWS, HD), 0, 1).reshape(TOK, HD)
    for part in range(TOK // HD):
        pick[:, part * HD : (part + 1) * HD] = jnp.where(source == lane + float(part * HD), 1.0, 0.0).astype(
            jnp.bfloat16
        )

    with jax.named_scope("W_upper"):
        for step in range(1, SIDE):
            pl.when(jnp.logical_and(step > rank, mover))(functools.partial(send_kv_known, step))
        for step in range(1, SIDE):
            pl.when(step > z)(functools.partial(send_q_known, step))
        for step in range(1, SIDE):
            pl.when(jnp.logical_and(step > rank, jnp.logical_not(mover)))(
                functools.partial(pl.semaphore_wait, known_y.at[step], 1)
            )

    low, high = pl.ds(0, SHARD // 2), pl.ds(SHARD // 2, SHARD // 2)
    with jax.named_scope("W_ring01"):
        ring[0].wait_recv()
        ring[1].wait_recv()
    ring.append(push(stored.at[left, low], stored.at[left, low], ring_send.at[3], ring_recv.at[3], tp=right))
    ring.append(push(stored.at[right, high], stored.at[right, high], ring_send.at[4], ring_recv.at[4], tp=left))
    ring.append(push(stored.at[left], stored.at[left], ring_send.at[5], ring_recv.at[5], tp=other))
    ring.append(push(stored.at[right], stored.at[right], ring_send.at[6], ring_recv.at[6], tp=other))

    own_pair = pltpu.make_async_copy(kv_mid.at[:, z], kv_all.at[:, z], loc_sem.at[1])

    def spread_span():
        with jax.named_scope("W_kv1"):
            own_kv.wait()
            await_all(kv_mid.at[pl.ds(0, SIDE - 1)], recv_sem.at[1])
        for d in FAR_FIRST:
            push(kv_mid.at[:, zs[d]], kv_all.at[:, z], send_sem.at[3], piece_sem.at[z], seq=y * SIDE + zs[d])
        own_pair.start()

    pl.when(mover)(spread_span)

    with jax.named_scope("W_q1"):
        own_q.wait()
        await_all(q_mid.at[pl.ds(0, SIDE - 1)], recv_sem.at[0])
    for d in FAR_FIRST:
        push(q_mid.at[:, ys[d]], q_all.at[y], send_sem.at[2], recv_sem.at[2], seq=ys[d] * SIDE + z)
    own_q = take(q_mid.at[:, y], q_all.at[y], loc_sem.at[0])

    with jax.named_scope("W_ring34"):
        ring[3].wait_recv()
        ring[4].wait_recv()
    ring.append(push(stored.at[far], stored.at[far], ring_send.at[7], ring_recv.at[7], tp=other))

    def hand_over():
        for step in range(SIDE):
            piece = kv_all.at[:, step]
            with jax.named_scope("W_kv2"):
                pl.when(step == z)(own_pair.wait)
                pl.when(step != z)(functools.partial(await_all, piece, piece_sem.at[step]))
            push(piece, piece, send_sem.at[5], recv_sem.at[3], tp=other)

    pl.when(mover)(hand_over)

    with jax.named_scope("W_q2"):
        own_q.wait()
        await_all(q_all.at[pl.ds(0, SIDE - 1)], recv_sem.at[2])
    with jax.named_scope("W_ringall"):
        own_shard.wait()
        for step in (2, 5, 6, 7):
            ring[step].wait_recv()

    rate = math.log2(math.e) / math.sqrt(HD)
    contract = (((1,), (1,)), ((), ()))
    block = 2 * GROUP
    keys = RING * 2 * SHARD
    limit = plen[z]
    live = slen[z]

    def cache_scores(number):
        rows = slice(number * block, (number + 1) * block)
        rows_q = jnp.dot(pick[rows, :], q_all[...].reshape(TOK, HD), preferred_element_type=jnp.float32)
        rows_q = rows_q.astype(jnp.bfloat16)
        q_tab[rows, :] = rows_q
        scores = lax.dot_general(
            rows_q, stored[:, :, :HD].reshape(keys, HD), contract, preferred_element_type=jnp.float32
        )
        seen = lax.broadcasted_iota(jnp.int32, (block, keys), 1) < limit
        return jnp.where(seen, scores, -jnp.inf)

    def tokens(number, width):
        count = lax.broadcasted_iota(jnp.int32, (block, width), 0)
        in_group = lax.bitwise_and(count, GROUP - 1)
        return (in_group - lax.bitwise_and(in_group, ROWS - 1)) * SIDE + (
            lax.bitwise_and(in_group, ROWS - 1) + ((count - in_group) // SIDE + 2 * number * ROWS)
        )

    def span_scores(number):
        rows = q_tab[number * block : (number + 1) * block, :]
        scores = lax.dot_general(
            rows, kv_all[:, :, :, :HD].reshape(TOK, HD), contract, preferred_element_type=jnp.float32
        )
        return jnp.where(place <= tokens(number, TOK).astype(jnp.float32), scores, -jnp.inf)

    def send_out(to, d):
        push(att.at[to, ys[d]], out_ref.at[s], send_sem.at[4], recv_sem.at[4], seq=ys[d] * SIDE + to)

    def attend(number, held, fresh):
        top = jnp.maximum(jnp.max(held, axis=1, keepdims=True), jnp.max(fresh, axis=1, keepdims=True))
        held = jnp.exp2((held - top) * rate).astype(jnp.bfloat16)
        fresh = jnp.exp2((fresh - top) * rate).astype(jnp.bfloat16)
        values = jnp.concatenate([stored[:, :, HD:].reshape(keys, HD), jnp.ones((keys, HD), jnp.bfloat16)], axis=1)
        total = jnp.dot(held, values, preferred_element_type=jnp.float32)
        values = jnp.concatenate([kv_all[:, :, :, HD:].reshape(TOK, HD), jnp.ones((TOK, HD), jnp.bfloat16)], axis=1)
        total = total + jnp.dot(fresh, values, preferred_element_type=jnp.float32)
        result = total[:, :HD] / total[:, HD:]
        result = jnp.where(tokens(number, HD) < live, result, 0.0).astype(jnp.bfloat16)
        att[2 * number : 2 * number + 2] = result.reshape(2, SIDE, ROWS, HD)
        for to in (2 * number, 2 * number + 1):
            for d in FAR_FIRST:
                send_out(to, d)
            pl.when(to != z)(functools.partial(send_out, to, 0))

    with jax.named_scope("C_cache0"):
        held = cache_scores(0)
    with jax.named_scope("W_swap"):
        pl.when(jnp.logical_not(mover))(functools.partial(await_all, kv_all, recv_sem.at[3]))
    fresh = span_scores(0)
    for number in range(TOK // block):
        with jax.named_scope(f"C_block{number}"):
            last = number == TOK // block - 1
            following = None if last else (cache_scores(number + 1), span_scores(number + 1))
            attend(number, held, fresh)
            if not last:
                held, fresh = following
    own = take(att.at[z, y], out_ref.at[s], loc_sem.at[0])

    for step in range(8):
        ring[step].wait_send()
    def span_sent():
        await_all(kv_all, send_sem.at[5])
        await_all(kv_mid.at[pl.ds(0, SIDE - 1)], send_sem.at[1])
        await_all(kv_mid.at[pl.ds(0, SIDE - 1)], send_sem.at[3])

    pl.when(mover)(span_sent)
    await_all(q_all.at[pl.ds(0, SIDE - 1)], send_sem.at[0])
    await_all(q_all.at[pl.ds(0, SIDE - 1)], send_sem.at[2])
    own.wait()
    peers = pl.ds(0, SIDE * SIDE - 1)
    with jax.named_scope("W_outsend"):
        await_all(out_ref.at[peers], send_sem.at[4])
    with jax.named_scope("W_out"):
        await_all(out_ref.at[peers], recv_sem.at[4])


def on_device(queries, span_kv, cache, prefix_len, span_len, row_source):
    shape = queries.shape
    hbm = pl.BlockSpec(memory_space=pl.ANY)
    tile = (SIDE, SIDE, ROWS, HD)
    out = pl.pallas_call(
        kernel,
        out_shape=pltpu.VMEM((SIDE * SIDE, ROWS, HD), jnp.bfloat16),
        in_specs=[hbm] * 6,
        out_specs=pl.BlockSpec(memory_space=pltpu.VMEM),
        scratch_shapes=[
            pltpu.VMEM(tile, jnp.bfloat16),
            pltpu.VMEM(tile, jnp.bfloat16),
            pltpu.VMEM((SIDE, SIDE, ROWS, 2 * HD), jnp.bfloat16),
            pltpu.VMEM((SIDE, SIDE, ROWS, 2 * HD), jnp.bfloat16),
            pltpu.VMEM((RING * 2, SHARD, 2 * HD), jnp.bfloat16),
            pltpu.SMEM((8,), jnp.int32),
            pltpu.SMEM((8,), jnp.int32),
            pltpu.VMEM((8, TOK), jnp.int32),
            pltpu.VMEM((TOK, TOK), jnp.bfloat16),
            pltpu.VMEM((TOK, HD), jnp.bfloat16),
            pltpu.VMEM(tile, jnp.bfloat16),
            pltpu.SemaphoreType.REGULAR((SIDE,)),
            pltpu.SemaphoreType.REGULAR((SIDE,)),
            pltpu.SemaphoreType.DMA((6,)),
            pltpu.SemaphoreType.DMA((6,)),
            pltpu.SemaphoreType.DMA((5,)),
            pltpu.SemaphoreType.DMA((SIDE,)),
            pltpu.SemaphoreType.DMA((8,)),
            pltpu.SemaphoreType.DMA((8,)),
        ],
        compiler_params=pltpu.CompilerParams(collective_id=0, has_side_effects=True),
    )(
        queries.reshape(tile),
        span_kv,
        cache,
        prefix_len,
        span_len,
        row_source,
    )
    return out.reshape(shape)


def solution(mesh):
    in_specs = (
        P(None, None, "seq", "tp", None),
        P(None, None, "seq", None),
        P("seq", "tp", None),
        P(),
        P(),
        P(),
    )
    out_specs = P(None, None, "seq", "tp", None)
    return jax.shard_map(on_device, mesh=mesh, in_specs=in_specs, out_specs=out_specs, check_vma=False)
```

```python
import functools
import math

import jax
import jax.numpy as jnp
from jax import lax
from jax.experimental import pallas as pl
from jax.experimental.pallas import tpu as pltpu
from jax.sharding import PartitionSpec as P

MESH = pl.DeviceIdType.MESH
SIDE = 8
RING = 4
ROWS = 8
HD = 128
TOK = 512
SHARD = 256
EARLY = 4
GROUP = 64
FAR_FIRST = (4, 3, 5, 2, 6, 1, 7)
BLOCKS = ((0, 2), (2, 4), (4, 6), (6, 8))
Y_ORDER = (0, 1, 2, 3, 7, 6, 5, 4)


def kernel(
    q_hbm,
    kv_hbm,
    cache_hbm,
    plen_hbm,
    slen_hbm,
    rs_hbm,
    out_ref,
    q_mid,
    q_up,
    q_all,
    kv_mid,
    kv_up,
    kv_all,
    stored,
    plen,
    slen,
    rs,
    pick,
    q_tab,
    att,
    known_y,
    known_z,
    q_bytes,
    loc_sem,
    z_send,
    z_recv,
    up_send,
    up_recv,
    y_send,
    far_send,
    q_done,
    low_done,
    high_done,
    swap_send,
    swap_recv,
    out_send,
    out_recv,
    ring_send,
    ring_recv,
):
    s = lax.axis_index("seq")
    t = lax.axis_index("tp")
    y, z = s // SIDE, s % SIDE
    x, core = t // 2, t % 2
    other = x * 2 + 1 - core
    x_right, x_left, x_far = lax.rem(x + 1, RING), lax.rem(x + RING - 1, RING), lax.rem(x + 2, RING)
    right, left, far = x_right * 2 + core, x_left * 2 + core, x_far * 2 + core
    ys = [lax.rem(y + d, SIDE) for d in range(SIDE)]

    rank = jnp.where(y < SIDE // 2, y, SIDE + SIDE // 2 - 1 - y)

    def signal(semaphore, **where):
        pl.semaphore_signal(semaphore, inc=1, device_id=where, device_id_type=MESH)

    barrier = pltpu.get_barrier_semaphore()
    for peer in (other, right, left):
        signal(barrier, tp=peer)
    for step in range(1, SIDE):
        pl.when(step > z)(functools.partial(signal, barrier, seq=y * SIDE + step))
        pl.when(step > rank)(functools.partial(signal, barrier, seq=Y_ORDER[step] * SIDE + z))
    with jax.named_scope("W_barrier"):
        pl.semaphore_wait(barrier, z + rank + 3)
    for step in range(SIDE - 1):
        pl.when(step < z)(functools.partial(signal, known_z.at[z], seq=y * SIDE + step))
        pl.when(step < rank)(functools.partial(signal, known_y.at[rank], seq=Y_ORDER[step] * SIDE + z))

    def push(src, dst, send, recv, **where):
        copy = pltpu.make_async_remote_copy(
            src_ref=src, dst_ref=dst, send_sem=send, recv_sem=recv, device_id=where, device_id_type=MESH
        )
        copy.start()
        return copy

    def take(src, dst, sem):
        copy = pltpu.make_async_copy(src, dst, sem)
        copy.start()
        return copy

    def await_all(ref, sem):
        pltpu.make_async_copy(ref, ref, sem).wait()

    mover = core == 1
    early, late = z < EARLY, z >= EARLY
    low_z, high_z = pl.ds(0, EARLY), pl.ds(EARLY, EARLY)
    queries = (0, q_hbm, q_mid, q_up, q_all)
    span = (1, kv_hbm, kv_mid, kv_up, kv_all)

    def streams(step, *args):
        step(*queries, *args)
        pl.when(mover)(functools.partial(step, *span, *args))

    def at_z(to):
        return {"seq": y * SIDE + to}

    def at_y(to):
        return {"seq": to * SIDE + z}

    def send_z(i, src, mid, up, every, to):
        push(src.at[:, to], mid.at[z], z_send.at[i], z_recv.at[i, z // EARLY], **at_z(to))

    def send_z_known(to):
        pl.semaphore_wait(known_z.at[to], 1)
        streams(send_z, to)

    def send_up(i, src, mid, up, every, to):
        push(src.at[to, high_z], up.at[y], up_send.at[i], up_recv.at[i], **at_y(to))

    def send_up_known(step):
        pl.semaphore_wait(known_y.at[step], 1)
        streams(send_up, Y_ORDER[step])

    def own_start(i, src, mid, up, every):
        pltpu.make_async_copy(src.at[:, z], mid.at[z], loc_sem.at[2 * i]).start()
        pl.when(early)(pltpu.make_async_copy(src.at[y, high_z], up.at[y], loc_sem.at[2 * i + 1]).start)

    for step in range(SIDE - 1):
        pl.when(step < z)(functools.partial(streams, send_z, step))
    for step in range(SIDE - 1):
        pl.when(jnp.logical_and(early, step < rank))(functools.partial(streams, send_up, Y_ORDER[step]))
    streams(own_start)

    shard = cache_hbm.at[0]
    ring = [
        push(shard, stored.at[t], ring_send.at[0], ring_recv.at[0], tp=right),
        push(shard, stored.at[t], ring_send.at[1], ring_recv.at[1], tp=left),
        push(shard, stored.at[t], ring_send.at[2], ring_recv.at[2], tp=other),
    ]
    own_shard = take(shard, stored.at[t], loc_sem.at[4])
    small = [
        take(plen_hbm, plen, loc_sem.at[5]),
        take(slen_hbm, slen, loc_sem.at[6]),
        take(rs_hbm, rs, loc_sem.at[7]),
    ]
    for load in small:
        load.wait()

    source = rs[pl.ds(z, 1), :].astype(jnp.float32)
    source = jnp.broadcast_to(source, (HD, TOK)).T
    row = lax.broadcasted_iota(jnp.int32, (TOK, HD), 0).astype(jnp.float32)
    lane = lax.broadcasted_iota(jnp.int32, (TOK, HD), 1).astype(jnp.float32)
    places = [
        jnp.sum(jnp.where(source == lane + float(part * HD), row, 0.0), axis=0, keepdims=True)
        for part in range(TOK // HD)
    ]
    place = jnp.concatenate(places, axis=1)
    source = jnp.swapaxes(source.reshape(SIDE, SIDE, ROWS, HD), 0, 1).reshape(TOK, HD)
    for part in range(TOK // HD):
        pick[:, part * HD : (part + 1) * HD] = jnp.where(source == lane + float(part * HD), 1.0, 0.0).astype(
            jnp.bfloat16
        )

    with jax.named_scope("W_upper"):
        for step in range(1, SIDE):
            pl.when(jnp.logical_and(early, step > rank))(functools.partial(send_up_known, step))
        for step in range(1, SIDE):
            open_now = step > z if step < EARLY else jnp.logical_and(late, step > z)
            pl.when(open_now)(functools.partial(send_z_known, step))
        for step in range(1, SIDE):
            pl.when(jnp.logical_and(late, step > rank))(
                functools.partial(pl.semaphore_wait, known_y.at[step], 1)
            )

    low, high = pl.ds(0, SHARD // 2), pl.ds(SHARD // 2, SHARD // 2)
    with jax.named_scope("W_ring01"):
        ring[0].wait_recv()
        ring[1].wait_recv()
    ring.append(push(stored.at[left, low], stored.at[left, low], ring_send.at[3], ring_recv.at[3], tp=right))
    ring.append(push(stored.at[right, high], stored.at[right, high], ring_send.at[4], ring_recv.at[4], tp=left))
    ring.append(push(stored.at[left], stored.at[left], ring_send.at[5], ring_recv.at[5], tp=other))
    ring.append(push(stored.at[right], stored.at[right], ring_send.at[6], ring_recv.at[6], tp=other))

    def send_y(i, src, mid, up, every, part, which, semaphores):
        for d in FAR_FIRST:
            push(mid.at[part, ys[d]], every.at[y, part], y_send.at[i, which], semaphores[i], **at_y(ys[d]))

    def own_wait(i, src, mid, up, every):
        pltpu.make_async_copy(src.at[:, z], mid.at[z], loc_sem.at[2 * i]).wait()

    def low_part(i, src, mid, up, every):
        with jax.named_scope("W_low"):
            own_wait(i, src, mid, up, every)
            await_all(mid.at[pl.ds(0, EARLY - 1)], z_recv.at[i, 0])
        send_y(i, src, mid, up, every, low_z, 0, (q_done, low_done))
        take(mid.at[low_z, y], every.at[y, low_z], loc_sem.at[2 * i])

    def up_wait(i, src, mid, up, every):
        with jax.named_scope("W_up"):
            pltpu.make_async_copy(src.at[y, high_z], up.at[y], loc_sem.at[2 * i + 1]).wait()
            await_all(up.at[pl.ds(0, SIDE - 1)], up_recv.at[i])

    def up_part(i, src, mid, up, every, to):
        push(up.at[:, to - EARLY], every.at[:, z], far_send.at[i], (q_done, low_done)[i], **at_z(to))

    def early_part():
        streams(low_part)
        streams(up_wait)
        for to in range(EARLY, SIDE):
            with jax.named_scope("W_far"):
                pl.semaphore_wait(known_z.at[to], 1)
            streams(up_part, to)

    pl.when(early)(early_part)

    def high_part(i, src, mid, up, every):
        with jax.named_scope("W_high"):
            pl.when(late)(functools.partial(own_wait, i, src, mid, up, every))
            pl.when(late)(functools.partial(await_all, mid.at[pl.ds(0, EARLY - 1)], z_recv.at[i, 1]))
            pl.when(early)(functools.partial(await_all, mid.at[pl.ds(0, EARLY)], z_recv.at[i, 1]))
        send_y(i, src, mid, up, every, high_z, 1, (q_done, high_done.at[y]))
        take(mid.at[high_z, y], every.at[y, high_z], loc_sem.at[2 * i + 1])

    streams(high_part)

    with jax.named_scope("W_ring34"):
        ring[3].wait_recv()
        ring[4].wait_recv()
    ring.append(push(stored.at[far], stored.at[far], ring_send.at[7], ring_recv.at[7], tp=other))

    def own_low_wait(i, src, mid, up, every):
        pltpu.make_async_copy(mid.at[low_z, y], every.at[y, low_z], loc_sem.at[2 * i]).wait()

    def own_high_wait(i, src, mid, up, every):
        pltpu.make_async_copy(mid.at[high_z, y], every.at[y, high_z], loc_sem.at[2 * i + 1]).wait()

    def hand_over():
        with jax.named_scope("W_kvlow"):
            pl.when(early)(functools.partial(own_low_wait, *span))
            pl.when(early)(functools.partial(await_all, kv_all.at[pl.ds(0, SIDE - 1), low_z], low_done))
            pl.when(late)(functools.partial(await_all, kv_all.at[:, low_z], low_done))
        push(kv_all.at[:, low_z], kv_all.at[:, low_z], swap_send, swap_recv, tp=other)
        for step in Y_ORDER:
            piece = kv_all.at[step, high_z]
            with jax.named_scope("W_kv2"):
                pl.when(step == y)(functools.partial(own_high_wait, *span))
                pl.when(step != y)(functools.partial(await_all, piece, high_done.at[step]))
            push(piece, piece, swap_send, swap_recv, tp=other)

    pl.when(mover)(hand_over)

    def early_queries():
        own_low_wait(*queries)
        await_all(q_all.at[pl.ds(0, SIDE - 1)], q_done)

    def late_queries():
        await_all(q_bytes, q_done)

    with jax.named_scope("W_q2"):
        own_high_wait(*queries)
        pl.when(early)(early_queries)
        pl.when(late)(late_queries)
    with jax.named_scope("W_ringall"):
        own_shard.wait()
        for step in (2, 5, 6, 7):
            ring[step].wait_recv()

    rate = math.log2(math.e) / math.sqrt(HD)
    contract = (((1,), (1,)), ((), ()))
    keys = RING * 2 * SHARD
    limit = plen[z]
    live = slen[z]

    def cache_scores(groups):
        rows = slice(groups[0] * GROUP, groups[1] * GROUP)
        rows_q = jnp.dot(pick[rows, :], q_all[...].reshape(TOK, HD), preferred_element_type=jnp.float32)
        rows_q = rows_q.astype(jnp.bfloat16)
        q_tab[rows, :] = rows_q
        scores = lax.dot_general(
            rows_q, stored[:, :, :HD].reshape(keys, HD), contract, preferred_element_type=jnp.float32
        )
        seen = lax.broadcasted_iota(jnp.int32, scores.shape, 1) < limit
        return jnp.where(seen, scores, -jnp.inf)

    def tokens(groups, width):
        count = lax.broadcasted_iota(jnp.int32, ((groups[1] - groups[0]) * GROUP, width), 0)
        in_group = lax.bitwise_and(count, GROUP - 1)
        return (in_group - lax.bitwise_and(in_group, ROWS - 1)) * SIDE + (
            lax.bitwise_and(in_group, ROWS - 1) + ((count - in_group) // SIDE + groups[0] * ROWS)
        )

    def span_scores(groups):
        rows = q_tab[groups[0] * GROUP : groups[1] * GROUP, :]
        scores = lax.dot_general(
            rows, kv_all[:, :, :, :HD].reshape(TOK, HD), contract, preferred_element_type=jnp.float32
        )
        return jnp.where(place <= tokens(groups, TOK).astype(jnp.float32), scores, -jnp.inf)

    def send_out(to, d):
        push(att.at[to, ys[d]], out_ref.at[s], out_send, out_recv, seq=ys[d] * SIDE + to)

    def attend(groups, held, fresh):
        top = jnp.maximum(jnp.max(held, axis=1, keepdims=True), jnp.max(fresh, axis=1, keepdims=True))
        held = jnp.exp2((held - top) * rate).astype(jnp.bfloat16)
        fresh = jnp.exp2((fresh - top) * rate).astype(jnp.bfloat16)
        values = jnp.concatenate([stored[:, :, HD:].reshape(keys, HD), jnp.ones((keys, HD), jnp.bfloat16)], axis=1)
        total = jnp.dot(held, values, preferred_element_type=jnp.float32)
        values = jnp.concatenate([kv_all[:, :, :, HD:].reshape(TOK, HD), jnp.ones((TOK, HD), jnp.bfloat16)], axis=1)
        total = total + jnp.dot(fresh, values, preferred_element_type=jnp.float32)
        result = total[:, :HD] / total[:, HD:]
        result = jnp.where(tokens(groups, HD) < live, result, 0.0).astype(jnp.bfloat16)
        att[groups[0] : groups[1]] = result.reshape(groups[1] - groups[0], SIDE, ROWS, HD)
        for to in range(*groups):
            for d in FAR_FIRST:
                send_out(to, d)
            pl.when(to != z)(functools.partial(send_out, to, 0))

    with jax.named_scope("C_cache0"):
        held = cache_scores(BLOCKS[0])
    with jax.named_scope("W_swap"):
        pl.when(jnp.logical_not(mover))(functools.partial(await_all, kv_all, swap_recv))
    fresh = span_scores(BLOCKS[0])
    for number, groups in enumerate(BLOCKS):
        with jax.named_scope(f"C_block{number}"):
            last = number == len(BLOCKS) - 1
            following = None if last else (cache_scores(BLOCKS[number + 1]), span_scores(BLOCKS[number + 1]))
            attend(groups, held, fresh)
            if not last:
                held, fresh = following
    own = take(att.at[z, y], out_ref.at[s], loc_sem.at[0])

    for step in range(8):
        ring[step].wait_send()
    def all_sent(i, src, mid, up, every):
        def early_sent():
            await_all(mid.at[pl.ds(0, EARLY - 1)], z_send.at[i])
            await_all(up.at[pl.ds(0, SIDE - 1)], up_send.at[i])
            await_all(up.at[pl.ds(0, SIDE - 1)], y_send.at[i, 0])
            await_all(mid.at[pl.ds(0, EARLY)], far_send.at[i])

        pl.when(early)(early_sent)
        pl.when(late)(functools.partial(await_all, mid.at[pl.ds(0, SIDE - 1)], z_send.at[i]))
        await_all(up.at[pl.ds(0, SIDE - 1)], y_send.at[i, 1])

    streams(all_sent)
    pl.when(mover)(functools.partial(await_all, kv_all, swap_send))
    own.wait()
    peers = pl.ds(0, SIDE * SIDE - 1)
    with jax.named_scope("W_outsend"):
        await_all(out_ref.at[peers], out_send)
    with jax.named_scope("W_out"):
        await_all(out_ref.at[peers], out_recv)


def on_device(queries, span_kv, cache, prefix_len, span_len, row_source):
    shape = queries.shape
    hbm = pl.BlockSpec(memory_space=pl.ANY)
    tile = (SIDE, SIDE, ROWS, HD)
    out = pl.pallas_call(
        kernel,
        out_shape=pltpu.VMEM((SIDE * SIDE, ROWS, HD), jnp.bfloat16),
        in_specs=[hbm] * 6,
        out_specs=pl.BlockSpec(memory_space=pltpu.VMEM),
        scratch_shapes=[
            pltpu.VMEM(tile, jnp.bfloat16),
            pltpu.VMEM((SIDE, EARLY, ROWS, HD), jnp.bfloat16),
            pltpu.VMEM(tile, jnp.bfloat16),
            pltpu.VMEM((SIDE, SIDE, ROWS, 2 * HD), jnp.bfloat16),
            pltpu.VMEM((SIDE, EARLY, ROWS, 2 * HD), jnp.bfloat16),
            pltpu.VMEM((SIDE, SIDE, ROWS, 2 * HD), jnp.bfloat16),
            pltpu.VMEM((RING * 2, SHARD, 2 * HD), jnp.bfloat16),
            pltpu.SMEM((8,), jnp.int32),
            pltpu.SMEM((8,), jnp.int32),
            pltpu.VMEM((8, TOK), jnp.int32),
            pltpu.VMEM((TOK, TOK), jnp.bfloat16),
            pltpu.VMEM((TOK, HD), jnp.bfloat16),
            pltpu.VMEM(tile, jnp.bfloat16),
            pltpu.SemaphoreType.REGULAR((SIDE,)),
            pltpu.SemaphoreType.REGULAR((SIDE,)),
            pltpu.VMEM((15, EARLY, ROWS, HD), jnp.bfloat16),
            pltpu.SemaphoreType.DMA((8,)),
            pltpu.SemaphoreType.DMA((2,)),
            pltpu.SemaphoreType.DMA((2, 2)),
            pltpu.SemaphoreType.DMA((2,)),
            pltpu.SemaphoreType.DMA((2,)),
            pltpu.SemaphoreType.DMA((2, 2)),
            pltpu.SemaphoreType.DMA((2,)),
            pltpu.SemaphoreType.DMA,
            pltpu.SemaphoreType.DMA,
            pltpu.SemaphoreType.DMA((SIDE,)),
            pltpu.SemaphoreType.DMA,
            pltpu.SemaphoreType.DMA,
            pltpu.SemaphoreType.DMA,
            pltpu.SemaphoreType.DMA,
            pltpu.SemaphoreType.DMA((8,)),
            pltpu.SemaphoreType.DMA((8,)),
        ],
        compiler_params=pltpu.CompilerParams(collective_id=0, has_side_effects=True),
    )(
        queries.reshape(tile),
        span_kv,
        cache,
        prefix_len,
        span_len,
        row_source,
    )
    return out.reshape(shape)


def solution(mesh):
    in_specs = (
        P(None, None, "seq", "tp", None),
        P(None, None, "seq", None),
        P("seq", "tp", None),
        P(),
        P(),
        P(),
    )
    out_specs = P(None, None, "seq", "tp", None)
    return jax.shard_map(on_device, mesh=mesh, in_specs=in_specs, out_specs=out_specs, check_vma=False)
```

```python
import functools
import math

import jax
import jax.numpy as jnp
from jax import lax
from jax.experimental import pallas as pl
from jax.experimental.pallas import tpu as pltpu
from jax.sharding import PartitionSpec as P

MESH = pl.DeviceIdType.MESH
SIDE = 8
RING = 4
ROWS = 8
HD = 128
TOK = 512
SHARD = 256
EARLY = 4
GROUP = 64
FAR_FIRST = (4, 3, 5, 2, 6, 1, 7)
BLOCKS = ((0, 2), (2, 4), (4, 6), (6, 8))
Y_ORDER = (0, 1, 2, 3, 7, 6, 5, 4)


def kernel(
    q_hbm,
    kv_hbm,
    cache_hbm,
    plen_hbm,
    slen_hbm,
    rs_hbm,
    out_ref,
    q_mid,
    q_up,
    q_all,
    kv_mid,
    kv_up,
    kv_all,
    stored,
    plen,
    slen,
    rs,
    pick,
    q_tab,
    att,
    known_y,
    known_z,
    q_bytes,
    loc_sem,
    z_send,
    z_recv,
    up_send,
    up_recv,
    y_send,
    far_send,
    q_done,
    low_done,
    high_done,
    swap_send,
    swap_recv,
    out_send,
    out_recv,
    ring_send,
    ring_recv,
):
    s = lax.axis_index("seq")
    t = lax.axis_index("tp")
    y, z = s // SIDE, s % SIDE
    x, core = t // 2, t % 2
    other = x * 2 + 1 - core
    x_right, x_left, x_far = lax.rem(x + 1, RING), lax.rem(x + RING - 1, RING), lax.rem(x + 2, RING)
    right, left, far = x_right * 2 + core, x_left * 2 + core, x_far * 2 + core
    ys = [lax.rem(y + d, SIDE) for d in range(SIDE)]

    rank = jnp.where(y < SIDE // 2, y, SIDE + SIDE // 2 - 1 - y)

    def signal(semaphore, **where):
        pl.semaphore_signal(semaphore, inc=1, device_id=where, device_id_type=MESH)

    barrier = pltpu.get_barrier_semaphore()
    for peer in (other, right, left):
        signal(barrier, tp=peer)
    for step in range(1, SIDE):
        pl.when(step > z)(functools.partial(signal, barrier, seq=y * SIDE + step))
        pl.when(step > rank)(functools.partial(signal, barrier, seq=Y_ORDER[step] * SIDE + z))
    with jax.named_scope("W_barrier"):
        pl.semaphore_wait(barrier, z + rank + 3)
    for step in range(SIDE - 1):
        pl.when(step < z)(functools.partial(signal, known_z.at[z], seq=y * SIDE + step))
        pl.when(step < rank)(functools.partial(signal, known_y.at[rank], seq=Y_ORDER[step] * SIDE + z))

    def push(src, dst, send, recv, **where):
        copy = pltpu.make_async_remote_copy(
            src_ref=src, dst_ref=dst, send_sem=send, recv_sem=recv, device_id=where, device_id_type=MESH
        )
        copy.start()
        return copy

    def take(src, dst, sem):
        copy = pltpu.make_async_copy(src, dst, sem)
        copy.start()
        return copy

    def await_all(ref, sem):
        pltpu.make_async_copy(ref, ref, sem).wait()

    mover = core == 1
    early, late = z < EARLY, z >= EARLY
    low_z, high_z = pl.ds(0, EARLY), pl.ds(EARLY, EARLY)
    queries = (0, q_hbm, q_mid, q_up, q_all)
    span = (1, kv_hbm, kv_mid, kv_up, kv_all)

    def streams(step, *args):
        pl.when(mover)(functools.partial(step, *span, *args))
        step(*queries, *args)

    def at_z(to):
        return {"seq": y * SIDE + to}

    def at_y(to):
        return {"seq": to * SIDE + z}

    def send_z(i, src, mid, up, every, to):
        push(src.at[:, to], mid.at[z], z_send.at[i], z_recv.at[i, z // EARLY], **at_z(to))

    def send_z_known(to):
        pl.semaphore_wait(known_z.at[to], 1)
        streams(send_z, to)

    def send_up(i, src, mid, up, every, to):
        push(src.at[to, high_z], up.at[y], up_send.at[i], up_recv.at[i], **at_y(to))

    def send_up_known(step):
        pl.semaphore_wait(known_y.at[step], 1)
        streams(send_up, Y_ORDER[step])

    def own_start(i, src, mid, up, every):
        pltpu.make_async_copy(src.at[:, z], mid.at[z], loc_sem.at[2 * i]).start()
        pl.when(early)(pltpu.make_async_copy(src.at[y, high_z], up.at[y], loc_sem.at[2 * i + 1]).start)

    for step in reversed(range(SIDE - 1)):
        pl.when(step < z)(functools.partial(streams, send_z, step))
    for step in range(SIDE - 1):
        pl.when(jnp.logical_and(early, step < rank))(functools.partial(streams, send_up, Y_ORDER[step]))
    streams(own_start)

    shard = cache_hbm.at[0]
    ring = [
        push(shard, stored.at[t], ring_send.at[0], ring_recv.at[0], tp=right),
        push(shard, stored.at[t], ring_send.at[1], ring_recv.at[1], tp=left),
        push(shard, stored.at[t], ring_send.at[2], ring_recv.at[2], tp=other),
    ]
    own_shard = take(shard, stored.at[t], loc_sem.at[4])
    small = [
        take(plen_hbm, plen, loc_sem.at[5]),
        take(slen_hbm, slen, loc_sem.at[6]),
        take(rs_hbm, rs, loc_sem.at[7]),
    ]
    for load in small:
        load.wait()

    source = rs[pl.ds(z, 1), :].astype(jnp.float32)
    source = jnp.broadcast_to(source, (HD, TOK)).T
    row = lax.broadcasted_iota(jnp.int32, (TOK, HD), 0).astype(jnp.float32)
    lane = lax.broadcasted_iota(jnp.int32, (TOK, HD), 1).astype(jnp.float32)
    places = [
        jnp.sum(jnp.where(source == lane + float(part * HD), row, 0.0), axis=0, keepdims=True)
        for part in range(TOK // HD)
    ]
    place = jnp.concatenate(places, axis=1)
    source = jnp.swapaxes(source.reshape(SIDE, SIDE, ROWS, HD), 0, 1).reshape(TOK, HD)
    for part in range(TOK // HD):
        pick[:, part * HD : (part + 1) * HD] = jnp.where(source == lane + float(part * HD), 1.0, 0.0).astype(
            jnp.bfloat16
        )

    with jax.named_scope("W_upper"):
        for step in range(1, SIDE):
            pl.when(jnp.logical_and(early, step > rank))(functools.partial(send_up_known, step))
        for step in range(1, SIDE):
            open_now = step > z if step < EARLY else jnp.logical_and(late, step > z)
            pl.when(open_now)(functools.partial(send_z_known, step))
        for step in range(1, SIDE):
            pl.when(jnp.logical_and(late, step > rank))(
                functools.partial(pl.semaphore_wait, known_y.at[step], 1)
            )

    low, high = pl.ds(0, SHARD // 2), pl.ds(SHARD // 2, SHARD // 2)
    with jax.named_scope("W_ring01"):
        ring[0].wait_recv()
        ring[1].wait_recv()
    ring.append(push(stored.at[left, low], stored.at[left, low], ring_send.at[3], ring_recv.at[3], tp=right))
    ring.append(push(stored.at[right, high], stored.at[right, high], ring_send.at[4], ring_recv.at[4], tp=left))
    ring.append(push(stored.at[left], stored.at[left], ring_send.at[5], ring_recv.at[5], tp=other))
    ring.append(push(stored.at[right], stored.at[right], ring_send.at[6], ring_recv.at[6], tp=other))

    def send_y(i, src, mid, up, every, part, which, semaphores):
        for d in FAR_FIRST:
            push(mid.at[part, ys[d]], every.at[y, part], y_send.at[i, which], semaphores[i], **at_y(ys[d]))

    def own_wait(i, src, mid, up, every):
        pltpu.make_async_copy(src.at[:, z], mid.at[z], loc_sem.at[2 * i]).wait()

    def low_part(i, src, mid, up, every):
        with jax.named_scope("W_low"):
            own_wait(i, src, mid, up, every)
            await_all(mid.at[pl.ds(0, EARLY - 1)], z_recv.at[i, 0])
        send_y(i, src, mid, up, every, low_z, 0, (q_done, low_done.at[y]))
        take(mid.at[low_z, y], every.at[y, low_z], loc_sem.at[2 * i])

    def up_wait(i, src, mid, up, every):
        with jax.named_scope("W_up"):
            pltpu.make_async_copy(src.at[y, high_z], up.at[y], loc_sem.at[2 * i + 1]).wait()
            await_all(up.at[pl.ds(0, SIDE - 1)], up_recv.at[i])

    def up_part(i, src, mid, up, every, to):
        push(up.at[:, to - EARLY], every.at[:, z], far_send.at[i], (q_done, low_done.at[z])[i], **at_z(to))

    def early_part():
        streams(low_part)
        streams(up_wait)
        for to in range(EARLY, SIDE):
            with jax.named_scope("W_far"):
                pl.semaphore_wait(known_z.at[to], 1)
            streams(up_part, to)

    pl.when(early)(early_part)

    def high_part(i, src, mid, up, every):
        with jax.named_scope("W_high"):
            pl.when(late)(functools.partial(own_wait, i, src, mid, up, every))
            pl.when(late)(functools.partial(await_all, mid.at[pl.ds(0, EARLY - 1)], z_recv.at[i, 1]))
            pl.when(early)(functools.partial(await_all, mid.at[pl.ds(0, EARLY)], z_recv.at[i, 1]))
        send_y(i, src, mid, up, every, high_z, 1, (q_done, high_done.at[y]))
        take(mid.at[high_z, y], every.at[y, high_z], loc_sem.at[2 * i + 1])

    streams(high_part)

    with jax.named_scope("W_ring34"):
        ring[3].wait_recv()
        ring[4].wait_recv()
    ring.append(push(stored.at[far], stored.at[far], ring_send.at[7], ring_recv.at[7], tp=other))

    def own_low_wait(i, src, mid, up, every):
        pltpu.make_async_copy(mid.at[low_z, y], every.at[y, low_z], loc_sem.at[2 * i]).wait()

    def own_high_wait(i, src, mid, up, every):
        pltpu.make_async_copy(mid.at[high_z, y], every.at[y, high_z], loc_sem.at[2 * i + 1]).wait()

    def hand(piece):
        push(piece, piece, swap_send, swap_recv, tp=other)

    def hand_low_y(step):
        piece = kv_all.at[step, low_z]
        with jax.named_scope("W_kvlow"):
            pl.when(step == y)(functools.partial(own_low_wait, *span))
            pl.when(step != y)(functools.partial(await_all, piece, low_done.at[step]))
        hand(piece)

    def hand_low_z(step):
        piece = kv_all.at[:, step]
        with jax.named_scope("W_kvlow"):
            await_all(piece, low_done.at[step])
        hand(piece)

    def hand_high(step):
        piece = kv_all.at[step, high_z]
        with jax.named_scope("W_kv2"):
            pl.when(step == y)(functools.partial(own_high_wait, *span))
            pl.when(step != y)(functools.partial(await_all, piece, high_done.at[step]))
        hand(piece)

    def hand_over_early():
        for step in Y_ORDER:
            hand_low_y(step)
        for step in Y_ORDER:
            hand_high(step)

    def hand_over_late():
        hand_low_z(0)
        for step in Y_ORDER[:4]:
            hand_high(step)
        hand_low_z(1)
        for step in Y_ORDER[4:]:
            hand_high(step)
        hand_low_z(2)
        hand_low_z(3)

    def hand_over():
        pl.when(early)(hand_over_early)
        pl.when(late)(hand_over_late)

    pl.when(mover)(hand_over)

    def early_queries():
        own_low_wait(*queries)
        await_all(q_all.at[pl.ds(0, SIDE - 1)], q_done)

    def late_queries():
        await_all(q_bytes, q_done)

    with jax.named_scope("W_q2"):
        own_high_wait(*queries)
        pl.when(early)(early_queries)
        pl.when(late)(late_queries)
    with jax.named_scope("W_ringall"):
        own_shard.wait()
        for step in (2, 5, 6, 7):
            ring[step].wait_recv()

    rate = math.log2(math.e) / math.sqrt(HD)
    contract = (((1,), (1,)), ((), ()))
    keys = RING * 2 * SHARD
    limit = plen[z]
    live = slen[z]

    def cache_scores(groups):
        rows = slice(groups[0] * GROUP, groups[1] * GROUP)
        rows_q = jnp.dot(pick[rows, :], q_all[...].reshape(TOK, HD), preferred_element_type=jnp.float32)
        rows_q = rows_q.astype(jnp.bfloat16)
        q_tab[rows, :] = rows_q
        scores = lax.dot_general(
            rows_q, stored[:, :, :HD].reshape(keys, HD), contract, preferred_element_type=jnp.float32
        )
        seen = lax.broadcasted_iota(jnp.int32, scores.shape, 1) < limit
        return jnp.where(seen, scores, -jnp.inf)

    def tokens(groups, width):
        count = lax.broadcasted_iota(jnp.int32, ((groups[1] - groups[0]) * GROUP, width), 0)
        in_group = lax.bitwise_and(count, GROUP - 1)
        return (in_group - lax.bitwise_and(in_group, ROWS - 1)) * SIDE + (
            lax.bitwise_and(in_group, ROWS - 1) + ((count - in_group) // SIDE + groups[0] * ROWS)
        )

    def span_scores(groups):
        rows = q_tab[groups[0] * GROUP : groups[1] * GROUP, :]
        scores = lax.dot_general(
            rows, kv_all[:, :, :, :HD].reshape(TOK, HD), contract, preferred_element_type=jnp.float32
        )
        return jnp.where(place <= tokens(groups, TOK).astype(jnp.float32), scores, -jnp.inf)

    def send_out(to, d):
        push(att.at[to, ys[d]], out_ref.at[s], out_send, out_recv, seq=ys[d] * SIDE + to)

    def attend(groups, held, fresh):
        top = jnp.maximum(jnp.max(held, axis=1, keepdims=True), jnp.max(fresh, axis=1, keepdims=True))
        held = jnp.exp2((held - top) * rate).astype(jnp.bfloat16)
        fresh = jnp.exp2((fresh - top) * rate).astype(jnp.bfloat16)
        values = jnp.concatenate([stored[:, :, HD:].reshape(keys, HD), jnp.ones((keys, HD), jnp.bfloat16)], axis=1)
        total = jnp.dot(held, values, preferred_element_type=jnp.float32)
        values = jnp.concatenate([kv_all[:, :, :, HD:].reshape(TOK, HD), jnp.ones((TOK, HD), jnp.bfloat16)], axis=1)
        total = total + jnp.dot(fresh, values, preferred_element_type=jnp.float32)
        result = total[:, :HD] / total[:, HD:]
        result = jnp.where(tokens(groups, HD) < live, result, 0.0).astype(jnp.bfloat16)
        att[groups[0] : groups[1]] = result.reshape(groups[1] - groups[0], SIDE, ROWS, HD)
        for to in range(*groups):
            for d in FAR_FIRST:
                send_out(to, d)
            pl.when(to != z)(functools.partial(send_out, to, 0))

    with jax.named_scope("C_cache0"):
        held = cache_scores(BLOCKS[0])
    with jax.named_scope("W_swap"):
        pl.when(jnp.logical_not(mover))(functools.partial(await_all, kv_all, swap_recv))
    fresh = span_scores(BLOCKS[0])
    for number, groups in enumerate(BLOCKS):
        with jax.named_scope(f"C_block{number}"):
            last = number == len(BLOCKS) - 1
            following = None if last else (cache_scores(BLOCKS[number + 1]), span_scores(BLOCKS[number + 1]))
            attend(groups, held, fresh)
            if not last:
                held, fresh = following
    own = take(att.at[z, y], out_ref.at[s], loc_sem.at[0])

    for step in range(8):
        ring[step].wait_send()
    def all_sent(i, src, mid, up, every):
        def early_sent():
            await_all(mid.at[pl.ds(0, EARLY - 1)], z_send.at[i])
            await_all(up.at[pl.ds(0, SIDE - 1)], up_send.at[i])
            await_all(up.at[pl.ds(0, SIDE - 1)], y_send.at[i, 0])
            await_all(mid.at[pl.ds(0, EARLY)], far_send.at[i])

        pl.when(early)(early_sent)
        pl.when(late)(functools.partial(await_all, mid.at[pl.ds(0, SIDE - 1)], z_send.at[i]))
        await_all(up.at[pl.ds(0, SIDE - 1)], y_send.at[i, 1])

    streams(all_sent)
    pl.when(mover)(functools.partial(await_all, kv_all, swap_send))
    own.wait()
    peers = pl.ds(0, SIDE * SIDE - 1)
    with jax.named_scope("W_outsend"):
        await_all(out_ref.at[peers], out_send)
    with jax.named_scope("W_out"):
        await_all(out_ref.at[peers], out_recv)


def on_device(queries, span_kv, cache, prefix_len, span_len, row_source):
    shape = queries.shape
    hbm = pl.BlockSpec(memory_space=pl.ANY)
    tile = (SIDE, SIDE, ROWS, HD)
    out = pl.pallas_call(
        kernel,
        out_shape=pltpu.VMEM((SIDE * SIDE, ROWS, HD), jnp.bfloat16),
        in_specs=[hbm] * 6,
        out_specs=pl.BlockSpec(memory_space=pltpu.VMEM),
        scratch_shapes=[
            pltpu.VMEM(tile, jnp.bfloat16),
            pltpu.VMEM((SIDE, EARLY, ROWS, HD), jnp.bfloat16),
            pltpu.VMEM(tile, jnp.bfloat16),
            pltpu.VMEM((SIDE, SIDE, ROWS, 2 * HD), jnp.bfloat16),
            pltpu.VMEM((SIDE, EARLY, ROWS, 2 * HD), jnp.bfloat16),
            pltpu.VMEM((SIDE, SIDE, ROWS, 2 * HD), jnp.bfloat16),
            pltpu.VMEM((RING * 2, SHARD, 2 * HD), jnp.bfloat16),
            pltpu.SMEM((8,), jnp.int32),
            pltpu.SMEM((8,), jnp.int32),
            pltpu.VMEM((8, TOK), jnp.int32),
            pltpu.VMEM((TOK, TOK), jnp.bfloat16),
            pltpu.VMEM((TOK, HD), jnp.bfloat16),
            pltpu.VMEM(tile, jnp.bfloat16),
            pltpu.SemaphoreType.REGULAR((SIDE,)),
            pltpu.SemaphoreType.REGULAR((SIDE,)),
            pltpu.VMEM((15, EARLY, ROWS, HD), jnp.bfloat16),
            pltpu.SemaphoreType.DMA((8,)),
            pltpu.SemaphoreType.DMA((2,)),
            pltpu.SemaphoreType.DMA((2, 2)),
            pltpu.SemaphoreType.DMA((2,)),
            pltpu.SemaphoreType.DMA((2,)),
            pltpu.SemaphoreType.DMA((2, 2)),
            pltpu.SemaphoreType.DMA((2,)),
            pltpu.SemaphoreType.DMA,
            pltpu.SemaphoreType.DMA((SIDE,)),
            pltpu.SemaphoreType.DMA((SIDE,)),
            pltpu.SemaphoreType.DMA,
            pltpu.SemaphoreType.DMA,
            pltpu.SemaphoreType.DMA,
            pltpu.SemaphoreType.DMA,
            pltpu.SemaphoreType.DMA((8,)),
            pltpu.SemaphoreType.DMA((8,)),
        ],
        compiler_params=pltpu.CompilerParams(collective_id=0, has_side_effects=True),
    )(
        queries.reshape(tile),
        span_kv,
        cache,
        prefix_len,
        span_len,
        row_source,
    )
    return out.reshape(shape)


def solution(mesh):
    in_specs = (
        P(None, None, "seq", "tp", None),
        P(None, None, "seq", None),
        P("seq", "tp", None),
        P(),
        P(),
        P(),
    )
    out_specs = P(None, None, "seq", "tp", None)
    return jax.shard_map(on_device, mesh=mesh, in_specs=in_specs, out_specs=out_specs, check_vma=False)
```

```python
import functools
import math

import jax
import jax.numpy as jnp
from jax import lax
from jax.experimental import pallas as pl
from jax.experimental.pallas import tpu as pltpu
from jax.sharding import PartitionSpec as P

MESH = pl.DeviceIdType.MESH
SIDE = 8
RING = 4
ROWS = 8
HD = 128
TOK = 512
SHARD = 256
EARLY = 4
EARLY_TILES = 3 * 8 + 3 * 7 * 4 + 4 * 8
LATE_TILES = 7 * 8 + 7 * 4
OTHER_TILES = 7 * 64 + 63
GROUP = 64
FAR_FIRST = (4, 3, 5, 2, 6, 1, 7)
BLOCKS = ((0, 2), (2, 4), (4, 6), (6, 8))
Y_ORDER = (0, 1, 2, 3, 7, 6, 5, 4)


def kernel(
    q_hbm,
    kv_hbm,
    cache_hbm,
    plen_hbm,
    slen_hbm,
    rs_hbm,
    out_ref,
    q_mid,
    q_up,
    q_all,
    kv_mid,
    kv_up,
    kv_all,
    stored,
    plen,
    slen,
    rs,
    pick,
    q_tab,
    att,
    known_y,
    known_z,
    nothing,
    loc_sem,
    sent,
    moved,
    z_recv,
    up_recv,
    q_done,
    low_done,
    high_done,
    swap_recv,
    out_recv,
    ring_recv,
):
    s = lax.axis_index("seq")
    t = lax.axis_index("tp")
    y, z = s // SIDE, s % SIDE
    x, core = t // 2, t % 2
    other = x * 2 + 1 - core
    x_right, x_left, x_far = lax.rem(x + 1, RING), lax.rem(x + RING - 1, RING), lax.rem(x + 2, RING)
    right, left, far = x_right * 2 + core, x_left * 2 + core, x_far * 2 + core
    ys = [lax.rem(y + d, SIDE) for d in range(SIDE)]

    rank = jnp.where(y < SIDE // 2, y, SIDE + SIDE // 2 - 1 - y)

    def signal(semaphore, **where):
        pl.semaphore_signal(semaphore, inc=1, device_id=where, device_id_type=MESH)

    barrier = pltpu.get_barrier_semaphore()
    for peer in (other, right, left):
        signal(barrier, tp=peer)
    for step in range(1, SIDE):
        pl.when(step > z)(functools.partial(signal, barrier, seq=y * SIDE + step))
        pl.when(step > rank)(functools.partial(signal, barrier, seq=Y_ORDER[step] * SIDE + z))
    with jax.named_scope("W_barrier"):
        pl.semaphore_wait(barrier, z + rank + 3)
    for step in range(SIDE - 1):
        pl.when(step < z)(functools.partial(signal, known_z.at[z], seq=y * SIDE + step))
        pl.when(step < rank)(functools.partial(signal, known_y.at[rank], seq=Y_ORDER[step] * SIDE + z))

    def push(src, dst, send, recv, **where):
        copy = pltpu.make_async_remote_copy(
            src_ref=src, dst_ref=dst, send_sem=send, recv_sem=recv, device_id=where, device_id_type=MESH
        )
        copy.start()
        return copy

    def take(src, dst, sem):
        copy = pltpu.make_async_copy(src, dst, sem)
        copy.start()
        return copy

    def await_all(ref, sem):
        pltpu.make_async_copy(ref, ref, sem).wait()

    mover = core == 1
    early, late = z < EARLY, z >= EARLY
    low_z, high_z = pl.ds(0, EARLY), pl.ds(EARLY, EARLY)
    queries = (0, q_hbm, q_mid, q_up, q_all)
    span = (1, kv_hbm, kv_mid, kv_up, kv_all)

    def streams(step, *args):
        pl.when(mover)(functools.partial(step, *span, *args))
        step(*queries, *args)

    def at_z(to):
        return {"seq": y * SIDE + to}

    def at_y(to):
        return {"seq": to * SIDE + z}

    def send_z(i, src, mid, up, every, to):
        push(src.at[:, to], mid.at[z], moved, z_recv.at[i, z // EARLY], **at_z(to))

    def send_z_known(to):
        pl.semaphore_wait(known_z.at[to], 1)
        streams(send_z, to)

    def send_up(i, src, mid, up, every, to):
        push(src.at[to, high_z], up.at[y], moved, up_recv.at[i], **at_y(to))

    def send_up_known(step):
        pl.semaphore_wait(known_y.at[step], 1)
        streams(send_up, Y_ORDER[step])

    def own_start(i, src, mid, up, every):
        pltpu.make_async_copy(src.at[:, z], mid.at[z], loc_sem.at[2 * i]).start()
        pl.when(early)(pltpu.make_async_copy(src.at[y, high_z], up.at[y], loc_sem.at[2 * i + 1]).start)

    for step in reversed(range(SIDE - 1)):
        pl.when(step < z)(functools.partial(streams, send_z, step))
    for step in range(SIDE - 1):
        pl.when(jnp.logical_and(early, step < rank))(functools.partial(streams, send_up, Y_ORDER[step]))
    streams(own_start)

    shard = cache_hbm.at[0]
    push(shard, stored.at[t], sent, ring_recv.at[0], tp=right)
    push(shard, stored.at[t], sent, ring_recv.at[0], tp=left)
    push(shard, stored.at[t], sent, ring_recv.at[2], tp=other)
    own_shard = take(shard, stored.at[t], loc_sem.at[4])
    small = [
        take(plen_hbm, plen, loc_sem.at[5]),
        take(slen_hbm, slen, loc_sem.at[6]),
        take(rs_hbm, rs, loc_sem.at[7]),
    ]
    for load in small:
        load.wait()

    source = rs[pl.ds(z, 1), :].astype(jnp.float32)
    source = jnp.broadcast_to(source, (HD, TOK)).T
    row = lax.broadcasted_iota(jnp.int32, (TOK, HD), 0).astype(jnp.float32)
    lane = lax.broadcasted_iota(jnp.int32, (TOK, HD), 1).astype(jnp.float32)
    places = [
        jnp.sum(jnp.where(source == lane + float(part * HD), row, 0.0), axis=0, keepdims=True)
        for part in range(TOK // HD)
    ]
    place = jnp.concatenate(places, axis=1)
    source = jnp.swapaxes(source.reshape(SIDE, SIDE, ROWS, HD), 0, 1).reshape(TOK, HD)
    for part in range(TOK // HD):
        pick[:, part * HD : (part + 1) * HD] = jnp.where(source == lane + float(part * HD), 1.0, 0.0).astype(
            jnp.bfloat16
        )

    with jax.named_scope("W_upper"):
        for step in range(1, SIDE):
            pl.when(jnp.logical_and(early, step > rank))(functools.partial(send_up_known, step))
        for step in range(1, SIDE):
            open_now = step > z if step < EARLY else jnp.logical_and(late, step > z)
            pl.when(open_now)(functools.partial(send_z_known, step))
        for step in range(1, SIDE):
            pl.when(jnp.logical_and(late, step > rank))(
                functools.partial(pl.semaphore_wait, known_y.at[step], 1)
            )

    low, high = pl.ds(0, SHARD // 2), pl.ds(SHARD // 2, SHARD // 2)
    with jax.named_scope("W_ring01"):
        await_all(stored.at[pl.ds(0, 2)], ring_recv.at[0])
    push(stored.at[left, low], stored.at[left, low], sent, ring_recv.at[1], tp=right)
    push(stored.at[right, high], stored.at[right, high], sent, ring_recv.at[1], tp=left)
    push(stored.at[left], stored.at[left], sent, ring_recv.at[2], tp=other)
    push(stored.at[right], stored.at[right], sent, ring_recv.at[2], tp=other)

    def send_y(i, src, mid, up, every, part, which, semaphores):
        for d in FAR_FIRST:
            push(mid.at[part, ys[d]], every.at[y, part], moved, semaphores[i], **at_y(ys[d]))

    def own_wait(i, src, mid, up, every):
        pltpu.make_async_copy(src.at[:, z], mid.at[z], loc_sem.at[2 * i]).wait()

    def low_part(i, src, mid, up, every):
        with jax.named_scope("W_low"):
            own_wait(i, src, mid, up, every)
            await_all(mid.at[pl.ds(0, EARLY - 1)], z_recv.at[i, 0])
        send_y(i, src, mid, up, every, low_z, 0, (q_done, low_done.at[0]))
        take(mid.at[low_z, y], every.at[y, low_z], loc_sem.at[2 * i])

    def up_wait(i, src, mid, up, every):
        with jax.named_scope("W_up"):
            pltpu.make_async_copy(src.at[y, high_z], up.at[y], loc_sem.at[2 * i + 1]).wait()
            await_all(up.at[pl.ds(0, SIDE - 1)], up_recv.at[i])

    def up_part(i, src, mid, up, every, to):
        push(up.at[:, to - EARLY], every.at[:, z], moved, (q_done, low_done.at[z])[i], **at_z(to))

    def early_part():
        streams(low_part)
        streams(up_wait)
        for to in range(EARLY, SIDE):
            with jax.named_scope("W_far"):
                pl.semaphore_wait(known_z.at[to], 1)
            streams(up_part, to)

    pl.when(early)(early_part)

    def high_part(i, src, mid, up, every):
        with jax.named_scope("W_high"):
            pl.when(late)(functools.partial(own_wait, i, src, mid, up, every))
            pl.when(late)(functools.partial(await_all, mid.at[pl.ds(0, EARLY - 1)], z_recv.at[i, 1]))
            pl.when(early)(functools.partial(await_all, mid.at[pl.ds(0, EARLY)], z_recv.at[i, 1]))
        send_y(i, src, mid, up, every, high_z, 1, (q_done, high_done.at[y]))
        take(mid.at[high_z, y], every.at[y, high_z], loc_sem.at[2 * i + 1])

    streams(high_part)

    with jax.named_scope("W_ring34"):
        await_all(stored.at[0], ring_recv.at[1])
    push(stored.at[far], stored.at[far], sent, ring_recv.at[2], tp=other)

    def own_low_wait(i, src, mid, up, every):
        pltpu.make_async_copy(mid.at[low_z, y], every.at[y, low_z], loc_sem.at[2 * i]).wait()

    def own_high_wait(i, src, mid, up, every):
        pltpu.make_async_copy(mid.at[high_z, y], every.at[y, high_z], loc_sem.at[2 * i + 1]).wait()

    def hand(piece):
        push(piece, piece, moved, swap_recv, tp=other)

    def hand_low_all():
        with jax.named_scope("W_kvlow"):
            own_low_wait(*span)
            await_all(kv_all.at[pl.ds(0, SIDE - 1), low_z], low_done.at[0])
        hand(kv_all.at[:, low_z])

    def hand_low_z(step):
        piece = kv_all.at[:, step]
        with jax.named_scope("W_kvlow"):
            await_all(piece, low_done.at[step])
        hand(piece)

    def hand_high(step):
        piece = kv_all.at[step, high_z]
        with jax.named_scope("W_kv2"):
            pl.when(step == y)(functools.partial(own_high_wait, *span))
            pl.when(step != y)(functools.partial(await_all, piece, high_done.at[step]))
        hand(piece)

    def hand_over_early():
        hand_low_all()
        for step in Y_ORDER:
            hand_high(step)

    def hand_over_late():
        hand_low_z(0)
        for step in Y_ORDER[:4]:
            hand_high(step)
        hand_low_z(1)
        for step in Y_ORDER[4:]:
            hand_high(step)
        hand_low_z(2)
        hand_low_z(3)

    def hand_over():
        pl.when(early)(hand_over_early)
        pl.when(late)(hand_over_late)

    pl.when(mover)(hand_over)

    def early_queries():
        own_low_wait(*queries)
        await_all(q_all.at[pl.ds(0, SIDE - 1)], q_done)

    def late_queries():
        await_all(nothing.at[pl.ds(0, (SIDE - 1) * EARLY + SIDE * EARLY)], q_done)

    with jax.named_scope("W_q2"):
        own_high_wait(*queries)
        pl.when(early)(early_queries)
        pl.when(late)(late_queries)
    with jax.named_scope("W_ringall"):
        own_shard.wait()
        await_all(stored.at[pl.ds(0, RING)], ring_recv.at[2])

    rate = math.log2(math.e) / math.sqrt(HD)
    contract = (((1,), (1,)), ((), ()))
    keys = RING * 2 * SHARD
    limit = plen[z]
    live = slen[z]

    def cache_scores(groups):
        rows = slice(groups[0] * GROUP, groups[1] * GROUP)
        rows_q = jnp.dot(pick[rows, :], q_all[...].reshape(TOK, HD), preferred_element_type=jnp.float32)
        rows_q = rows_q.astype(jnp.bfloat16)
        q_tab[rows, :] = rows_q
        scores = lax.dot_general(
            rows_q, stored[:, :, :HD].reshape(keys, HD), contract, preferred_element_type=jnp.float32
        )
        seen = lax.broadcasted_iota(jnp.int32, scores.shape, 1) < limit
        return jnp.where(seen, scores, -jnp.inf)

    def tokens(groups, width):
        count = lax.broadcasted_iota(jnp.int32, ((groups[1] - groups[0]) * GROUP, width), 0)
        in_group = lax.bitwise_and(count, GROUP - 1)
        return (in_group - lax.bitwise_and(in_group, ROWS - 1)) * SIDE + (
            lax.bitwise_and(in_group, ROWS - 1) + ((count - in_group) // SIDE + groups[0] * ROWS)
        )

    def span_scores(groups):
        rows = q_tab[groups[0] * GROUP : groups[1] * GROUP, :]
        scores = lax.dot_general(
            rows, kv_all[:, :, :, :HD].reshape(TOK, HD), contract, preferred_element_type=jnp.float32
        )
        return jnp.where(place <= tokens(groups, TOK).astype(jnp.float32), scores, -jnp.inf)

    def send_out(to, d):
        push(att.at[to, ys[d]], out_ref.at[s], sent, out_recv, seq=ys[d] * SIDE + to)

    def cache_part(held):
        top = jnp.max(held, axis=1, keepdims=True)
        held = jnp.exp2((held - top) * rate).astype(jnp.bfloat16)
        values = jnp.concatenate([stored[:, :, HD:].reshape(keys, HD), jnp.ones((keys, HD), jnp.bfloat16)], axis=1)
        return top, jnp.dot(held, values, preferred_element_type=jnp.float32)

    def span_part(fresh, top):
        fresh = jnp.exp2((fresh - top) * rate).astype(jnp.bfloat16)
        values = jnp.concatenate([kv_all[:, :, :, HD:].reshape(TOK, HD), jnp.ones((TOK, HD), jnp.bfloat16)], axis=1)
        return jnp.dot(fresh, values, preferred_element_type=jnp.float32)

    def attend(held, fresh):
        top = jnp.maximum(jnp.max(held, axis=1, keepdims=True), jnp.max(fresh, axis=1, keepdims=True))
        held = jnp.exp2((held - top) * rate).astype(jnp.bfloat16)
        values = jnp.concatenate([stored[:, :, HD:].reshape(keys, HD), jnp.ones((keys, HD), jnp.bfloat16)], axis=1)
        return jnp.dot(held, values, preferred_element_type=jnp.float32) + span_part(fresh, top)

    def attend_late(before, total, fresh):
        top = jnp.maximum(before, jnp.max(fresh, axis=1, keepdims=True))
        return total * jnp.exp2((before - top) * rate) + span_part(fresh, top)

    def finish(groups, total):
        result = total[:, :HD] / total[:, HD:]
        result = jnp.where(tokens(groups, HD) < live, result, 0.0).astype(jnp.bfloat16)
        att[groups[0] : groups[1]] = result.reshape(groups[1] - groups[0], SIDE, ROWS, HD)
        for to in range(*groups):
            for d in FAR_FIRST:
                send_out(to, d)
            pl.when(to != z)(functools.partial(send_out, to, 0))

    with jax.named_scope("C_cache0"):
        top, total = cache_part(cache_scores(BLOCKS[0]))
        held = [None] + [cache_scores(groups) for groups in BLOCKS[1:1]]
    with jax.named_scope("W_swap"):
        pl.when(jnp.logical_not(mover))(functools.partial(await_all, kv_all, swap_recv))
    fresh = span_scores(BLOCKS[0])
    for number, groups in enumerate(BLOCKS):
        with jax.named_scope(f"C_block{number}"):
            if number + 1 < len(BLOCKS):
                if number + 1 >= len(held):
                    held.append(cache_scores(BLOCKS[number + 1]))
                following = span_scores(BLOCKS[number + 1])
            if number == 0:
                total = attend_late(top, total, fresh)
            else:
                total = attend(held[number], fresh)
            finish(groups, total)
            fresh = following
    own = take(att.at[z, y], out_ref.at[s], loc_sem.at[0])

    await_all(nothing.at[pl.ds(0, OTHER_TILES)], sent)
    for rows, count in ((early, EARLY_TILES), (late, LATE_TILES)):
        mine = jnp.logical_and(rows, mover)
        pl.when(mine)(functools.partial(await_all, nothing.at[pl.ds(0, 3 * count + 128)], moved))
        mine = jnp.logical_and(rows, jnp.logical_not(mover))
        pl.when(mine)(functools.partial(await_all, nothing.at[pl.ds(0, count)], moved))
    own.wait()
    peers = pl.ds(0, SIDE * SIDE - 1)
    with jax.named_scope("W_out"):
        await_all(out_ref.at[peers], out_recv)


def on_device(queries, span_kv, cache, prefix_len, span_len, row_source):
    shape = queries.shape
    hbm = pl.BlockSpec(memory_space=pl.ANY)
    tile = (SIDE, SIDE, ROWS, HD)
    out = pl.pallas_call(
        kernel,
        out_shape=pltpu.VMEM((SIDE * SIDE, ROWS, HD), jnp.bfloat16),
        in_specs=[hbm] * 6,
        out_specs=pl.BlockSpec(memory_space=pltpu.VMEM),
        scratch_shapes=[
            pltpu.VMEM(tile, jnp.bfloat16),
            pltpu.VMEM((SIDE, EARLY, ROWS, HD), jnp.bfloat16),
            pltpu.VMEM(tile, jnp.bfloat16),
            pltpu.VMEM((SIDE, SIDE, ROWS, 2 * HD), jnp.bfloat16),
            pltpu.VMEM((SIDE, EARLY, ROWS, 2 * HD), jnp.bfloat16),
            pltpu.VMEM((SIDE, SIDE, ROWS, 2 * HD), jnp.bfloat16),
            pltpu.VMEM((RING * 2, SHARD, 2 * HD), jnp.bfloat16),
            pltpu.SMEM((8,), jnp.int32),
            pltpu.SMEM((8,), jnp.int32),
            pltpu.VMEM((8, TOK), jnp.int32),
            pltpu.VMEM((TOK, TOK), jnp.bfloat16),
            pltpu.VMEM((TOK, HD), jnp.bfloat16),
            pltpu.VMEM(tile, jnp.bfloat16),
            pltpu.SemaphoreType.REGULAR((SIDE,)),
            pltpu.SemaphoreType.REGULAR((SIDE,)),
            pltpu.VMEM((3 * EARLY_TILES + 128, ROWS, HD), jnp.bfloat16),
            pltpu.SemaphoreType.DMA((8,)),
            pltpu.SemaphoreType.DMA,
            pltpu.SemaphoreType.DMA,
            pltpu.SemaphoreType.DMA((2, 2)),
            pltpu.SemaphoreType.DMA((2,)),
            pltpu.SemaphoreType.DMA,
            pltpu.SemaphoreType.DMA((EARLY,)),
            pltpu.SemaphoreType.DMA((SIDE,)),
            pltpu.SemaphoreType.DMA,
            pltpu.SemaphoreType.DMA,
            pltpu.SemaphoreType.DMA((3,)),
        ],
        compiler_params=pltpu.CompilerParams(collective_id=0, has_side_effects=True),
    )(
        queries.reshape(tile),
        span_kv,
        cache,
        prefix_len,
        span_len,
        row_source,
    )
    return out.reshape(shape)


def solution(mesh):
    in_specs = (
        P(None, None, "seq", "tp", None),
        P(None, None, "seq", None),
        P("seq", "tp", None),
        P(),
        P(),
        P(),
    )
    out_specs = P(None, None, "seq", "tp", None)
    return jax.shard_map(on_device, mesh=mesh, in_specs=in_specs, out_specs=out_specs, check_vma=False)
```

```python
import functools
import math

import jax
import jax.numpy as jnp
from jax import lax
from jax.experimental import pallas as pl
from jax.experimental.pallas import tpu as pltpu
from jax.sharding import PartitionSpec as P

MESH = pl.DeviceIdType.MESH
SIDE = 8
RING = 4
ROWS = 8
HD = 128
TOK = 512
SHARD = 256
EARLY = 4
EARLY_TILES = 3 * 8 + 3 * 7 * 4 + 4 * 8
LATE_TILES = 7 * 8 + 7 * 4
OTHER_TILES = 7 * 64 + 63
GROUP = 64
FAR_FIRST = (4, 3, 5, 2, 6, 1, 7)
BLOCKS = ((0, 2), (2, 4), (4, 6), (6, 8))
Y_ORDER = (0, 1, 2, 3, 7, 6, 5, 4)


def kernel(
    q_hbm,
    kv_hbm,
    cache_hbm,
    plen_hbm,
    slen_hbm,
    rs_hbm,
    out_ref,
    q_mid,
    q_up,
    q_all,
    kv_mid,
    kv_up,
    kv_all,
    stored,
    plen,
    slen,
    rs,
    pick,
    q_tab,
    att,
    known_y,
    known_z,
    nothing,
    loc_sem,
    sent,
    moved,
    z_recv,
    up_recv,
    q_done,
    low_done,
    high_done,
    swap_recv,
    out_recv,
    ring_recv,
):
    s = lax.axis_index("seq")
    t = lax.axis_index("tp")
    y, z = s // SIDE, s % SIDE
    x, core = t // 2, t % 2
    other = x * 2 + 1 - core
    x_right, x_left, x_far = lax.rem(x + 1, RING), lax.rem(x + RING - 1, RING), lax.rem(x + 2, RING)
    right, left, far = x_right * 2 + core, x_left * 2 + core, x_far * 2 + core
    ys = [lax.rem(y + d, SIDE) for d in range(SIDE)]

    rank = jnp.where(y < SIDE // 2, y, SIDE + SIDE // 2 - 1 - y)

    def signal(semaphore, **where):
        pl.semaphore_signal(semaphore, inc=1, device_id=where, device_id_type=MESH)

    barrier = pltpu.get_barrier_semaphore()
    for peer in (other, right, left):
        signal(barrier, tp=peer)
    for step in range(1, SIDE):
        pl.when(step > z)(functools.partial(signal, barrier, seq=y * SIDE + step))
        pl.when(step > rank)(functools.partial(signal, barrier, seq=Y_ORDER[step] * SIDE + z))
    with jax.named_scope("W_barrier"):
        pl.semaphore_wait(barrier, z + rank + 3)
    for step in range(SIDE - 1):
        pl.when(step < z)(functools.partial(signal, known_z.at[z], seq=y * SIDE + step))
        pl.when(step < rank)(functools.partial(signal, known_y.at[rank], seq=Y_ORDER[step] * SIDE + z))

    def push(src, dst, send, recv, **where):
        copy = pltpu.make_async_remote_copy(
            src_ref=src, dst_ref=dst, send_sem=send, recv_sem=recv, device_id=where, device_id_type=MESH
        )
        copy.start()
        return copy

    def take(src, dst, sem):
        copy = pltpu.make_async_copy(src, dst, sem)
        copy.start()
        return copy

    def await_all(ref, sem):
        pltpu.make_async_copy(ref, ref, sem).wait()

    mover = core == 1
    early, late = z < EARLY, z >= EARLY
    low_z, high_z = pl.ds(0, EARLY), pl.ds(EARLY, EARLY)
    queries = (0, q_hbm, q_mid, q_up, q_all)
    span = (1, kv_hbm, kv_mid, kv_up, kv_all)

    def streams(step, *args):
        pl.when(mover)(functools.partial(step, *span, *args))
        step(*queries, *args)

    def at_z(to):
        return {"seq": y * SIDE + to}

    def at_y(to):
        return {"seq": to * SIDE + z}

    def send_z(i, src, mid, up, every, to):
        push(src.at[:, to], mid.at[z], moved, z_recv.at[i, z // EARLY], **at_z(to))

    def send_z_known(to):
        pl.semaphore_wait(known_z.at[to], 1)
        streams(send_z, to)

    def send_up(i, src, mid, up, every, to):
        push(src.at[to, high_z], up.at[y], moved, up_recv.at[i], **at_y(to))

    def send_up_known(step):
        pl.semaphore_wait(known_y.at[step], 1)
        streams(send_up, Y_ORDER[step])

    def own_start(i, src, mid, up, every):
        pltpu.make_async_copy(src.at[:, z], mid.at[z], loc_sem.at[2 * i]).start()
        pl.when(early)(pltpu.make_async_copy(src.at[y, high_z], up.at[y], loc_sem.at[2 * i + 1]).start)

    for step in reversed(range(SIDE - 1)):
        pl.when(step < z)(functools.partial(streams, send_z, step))
    for step in range(SIDE - 1):
        pl.when(jnp.logical_and(early, step < rank))(functools.partial(streams, send_up, Y_ORDER[step]))
    streams(own_start)

    shard = cache_hbm.at[0]
    push(shard, stored.at[t], sent, ring_recv.at[0], tp=right)
    push(shard, stored.at[t], sent, ring_recv.at[0], tp=left)
    push(shard, stored.at[t], sent, ring_recv.at[2], tp=other)
    own_shard = take(shard, stored.at[t], loc_sem.at[4])
    small = [
        take(plen_hbm, plen, loc_sem.at[5]),
        take(slen_hbm, slen, loc_sem.at[6]),
        take(rs_hbm, rs, loc_sem.at[7]),
    ]
    for load in small:
        load.wait()

    source = rs[pl.ds(z, 1), :].astype(jnp.float32)
    source = jnp.broadcast_to(source, (HD, TOK)).T
    row = lax.broadcasted_iota(jnp.int32, (TOK, HD), 0).astype(jnp.float32)
    lane = lax.broadcasted_iota(jnp.int32, (TOK, HD), 1).astype(jnp.float32)
    places = [
        jnp.sum(jnp.where(source == lane + float(part * HD), row, 0.0), axis=0, keepdims=True)
        for part in range(TOK // HD)
    ]
    place = jnp.concatenate(places, axis=1)
    source = jnp.swapaxes(source.reshape(SIDE, SIDE, ROWS, HD), 0, 1).reshape(TOK, HD)
    for part in range(TOK // HD):
        pick[:, part * HD : (part + 1) * HD] = jnp.where(source == lane + float(part * HD), 1.0, 0.0).astype(
            jnp.bfloat16
        )

    with jax.named_scope("W_upper"):
        for step in range(1, SIDE):
            pl.when(jnp.logical_and(early, step > rank))(functools.partial(send_up_known, step))
        for step in range(1, SIDE):
            open_now = step > z if step < EARLY else jnp.logical_and(late, step > z)
            pl.when(open_now)(functools.partial(send_z_known, step))
        for step in range(1, SIDE):
            pl.when(jnp.logical_and(late, step > rank))(
                functools.partial(pl.semaphore_wait, known_y.at[step], 1)
            )

    low, high = pl.ds(0, SHARD // 2), pl.ds(SHARD // 2, SHARD // 2)
    with jax.named_scope("W_ring01"):
        await_all(stored.at[pl.ds(0, 2)], ring_recv.at[0])
    push(stored.at[left, low], stored.at[left, low], sent, ring_recv.at[1], tp=right)
    push(stored.at[right, high], stored.at[right, high], sent, ring_recv.at[1], tp=left)
    push(stored.at[left], stored.at[left], sent, ring_recv.at[2], tp=other)
    push(stored.at[right], stored.at[right], sent, ring_recv.at[2], tp=other)

    def send_y(i, src, mid, up, every, part, which, semaphores):
        for d in FAR_FIRST:
            push(mid.at[part, ys[d]], every.at[y, part], moved, semaphores[i], **at_y(ys[d]))

    def own_wait(i, src, mid, up, every):
        pltpu.make_async_copy(src.at[:, z], mid.at[z], loc_sem.at[2 * i]).wait()

    def low_part(i, src, mid, up, every):
        with jax.named_scope("W_low"):
            own_wait(i, src, mid, up, every)
            await_all(mid.at[pl.ds(0, EARLY - 1)], z_recv.at[i, 0])
        send_y(i, src, mid, up, every, low_z, 0, (q_done, low_done.at[0]))
        take(mid.at[low_z, y], every.at[y, low_z], loc_sem.at[2 * i])

    def up_wait(i, src, mid, up, every):
        with jax.named_scope("W_up"):
            pltpu.make_async_copy(src.at[y, high_z], up.at[y], loc_sem.at[2 * i + 1]).wait()
            await_all(up.at[pl.ds(0, SIDE - 1)], up_recv.at[i])

    def up_part(i, src, mid, up, every, to):
        push(up.at[:, to - EARLY], every.at[:, z], moved, (q_done, low_done.at[z])[i], **at_z(to))

    def early_part():
        streams(low_part)
        streams(up_wait)
        for to in range(EARLY, SIDE):
            with jax.named_scope("W_far"):
                pl.semaphore_wait(known_z.at[to], 1)
            pl.when(mover)(functools.partial(up_part, *span, to))
        for to in range(EARLY, SIDE):
            up_part(*queries, to)

    pl.when(early)(early_part)

    def high_part(i, src, mid, up, every):
        with jax.named_scope("W_high"):
            pl.when(late)(functools.partial(own_wait, i, src, mid, up, every))
            pl.when(late)(functools.partial(await_all, mid.at[pl.ds(0, EARLY - 1)], z_recv.at[i, 1]))
            pl.when(early)(functools.partial(await_all, mid.at[pl.ds(0, EARLY)], z_recv.at[i, 1]))
        send_y(i, src, mid, up, every, high_z, 1, (q_done, high_done.at[y]))
        take(mid.at[high_z, y], every.at[y, high_z], loc_sem.at[2 * i + 1])

    streams(high_part)

    with jax.named_scope("W_ring34"):
        await_all(stored.at[0], ring_recv.at[1])
    push(stored.at[far], stored.at[far], sent, ring_recv.at[2], tp=other)

    def own_low_wait(i, src, mid, up, every):
        pltpu.make_async_copy(mid.at[low_z, y], every.at[y, low_z], loc_sem.at[2 * i]).wait()

    def own_high_wait(i, src, mid, up, every):
        pltpu.make_async_copy(mid.at[high_z, y], every.at[y, high_z], loc_sem.at[2 * i + 1]).wait()

    def hand(piece):
        push(piece, piece, moved, swap_recv, tp=other)

    def hand_low_all():
        with jax.named_scope("W_kvlow"):
            own_low_wait(*span)
            await_all(kv_all.at[pl.ds(0, SIDE - 1), low_z], low_done.at[0])
        hand(kv_all.at[:, low_z])

    def hand_low_z(step):
        piece = kv_all.at[:, step]
        with jax.named_scope("W_kvlow"):
            await_all(piece, low_done.at[step])
        hand(piece)

    def hand_high(step):
        piece = kv_all.at[step, high_z]
        with jax.named_scope("W_kv2"):
            pl.when(step == y)(functools.partial(own_high_wait, *span))
            pl.when(step != y)(functools.partial(await_all, piece, high_done.at[step]))
        hand(piece)

    def hand_over_early():
        hand_low_all()
        for step in Y_ORDER:
            hand_high(step)

    def hand_over_late():
        hand_low_z(0)
        for step in Y_ORDER[:4]:
            hand_high(step)
        hand_low_z(1)
        for step in Y_ORDER[4:]:
            hand_high(step)
        hand_low_z(2)
        hand_low_z(3)

    def hand_over():
        pl.when(early)(hand_over_early)
        pl.when(late)(hand_over_late)

    pl.when(mover)(hand_over)

    def early_queries():
        own_low_wait(*queries)
        await_all(q_all.at[pl.ds(0, SIDE - 1)], q_done)

    def late_queries():
        await_all(nothing.at[pl.ds(0, (SIDE - 1) * EARLY + SIDE * EARLY)], q_done)

    with jax.named_scope("W_q2"):
        own_high_wait(*queries)
        pl.when(early)(early_queries)
        pl.when(late)(late_queries)
    with jax.named_scope("W_ringall"):
        own_shard.wait()
        await_all(stored.at[pl.ds(0, RING)], ring_recv.at[2])

    rate = math.log2(math.e) / math.sqrt(HD)
    contract = (((1,), (1,)), ((), ()))
    keys = RING * 2 * SHARD
    limit = plen[z]
    live = slen[z]

    def cache_scores(groups):
        rows = slice(groups[0] * GROUP, groups[1] * GROUP)
        rows_q = jnp.dot(pick[rows, :], q_all[...].reshape(TOK, HD), preferred_element_type=jnp.float32)
        rows_q = rows_q.astype(jnp.bfloat16)
        q_tab[rows, :] = rows_q
        scores = lax.dot_general(
            rows_q, stored[:, :, :HD].reshape(keys, HD), contract, preferred_element_type=jnp.float32
        )
        seen = lax.broadcasted_iota(jnp.int32, scores.shape, 1) < limit
        return jnp.where(seen, scores, -jnp.inf)

    def tokens(groups, width):
        count = lax.broadcasted_iota(jnp.int32, ((groups[1] - groups[0]) * GROUP, width), 0)
        in_group = lax.bitwise_and(count, GROUP - 1)
        return (in_group - lax.bitwise_and(in_group, ROWS - 1)) * SIDE + (
            lax.bitwise_and(in_group, ROWS - 1) + ((count - in_group) // SIDE + groups[0] * ROWS)
        )

    def span_scores(groups):
        rows = q_tab[groups[0] * GROUP : groups[1] * GROUP, :]
        scores = lax.dot_general(
            rows, kv_all[:, :, :, :HD].reshape(TOK, HD), contract, preferred_element_type=jnp.float32
        )
        return jnp.where(place <= tokens(groups, TOK).astype(jnp.float32), scores, -jnp.inf)

    def send_out(to, d):
        push(att.at[to, ys[d]], out_ref.at[s], sent, out_recv, seq=ys[d] * SIDE + to)

    def cache_part(held):
        top = jnp.max(held, axis=1, keepdims=True)
        held = jnp.exp2((held - top) * rate).astype(jnp.bfloat16)
        values = jnp.concatenate([stored[:, :, HD:].reshape(keys, HD), jnp.ones((keys, HD), jnp.bfloat16)], axis=1)
        return top, jnp.dot(held, values, preferred_element_type=jnp.float32)

    def span_part(fresh, top):
        fresh = jnp.exp2((fresh - top) * rate).astype(jnp.bfloat16)
        values = jnp.concatenate([kv_all[:, :, :, HD:].reshape(TOK, HD), jnp.ones((TOK, HD), jnp.bfloat16)], axis=1)
        return jnp.dot(fresh, values, preferred_element_type=jnp.float32)

    def attend(held, fresh):
        top = jnp.maximum(jnp.max(held, axis=1, keepdims=True), jnp.max(fresh, axis=1, keepdims=True))
        held = jnp.exp2((held - top) * rate).astype(jnp.bfloat16)
        values = jnp.concatenate([stored[:, :, HD:].reshape(keys, HD), jnp.ones((keys, HD), jnp.bfloat16)], axis=1)
        return jnp.dot(held, values, preferred_element_type=jnp.float32) + span_part(fresh, top)

    def attend_late(before, total, fresh):
        top = jnp.maximum(before, jnp.max(fresh, axis=1, keepdims=True))
        return total * jnp.exp2((before - top) * rate) + span_part(fresh, top)

    def finish(groups, total):
        result = total[:, :HD] / total[:, HD:]
        result = jnp.where(tokens(groups, HD) < live, result, 0.0).astype(jnp.bfloat16)
        att[groups[0] : groups[1]] = result.reshape(groups[1] - groups[0], SIDE, ROWS, HD)
        for to in range(*groups):
            for d in FAR_FIRST:
                send_out(to, d)
            pl.when(to != z)(functools.partial(send_out, to, 0))

    with jax.named_scope("C_cache0"):
        top, total = cache_part(cache_scores(BLOCKS[0]))
        held = [None, cache_scores(BLOCKS[1])]
    with jax.named_scope("W_swap"):
        pl.when(jnp.logical_not(mover))(functools.partial(await_all, kv_all, swap_recv))
    with jax.named_scope("C_block0"):
        finish(BLOCKS[0], attend_late(top, total, span_scores(BLOCKS[0])))
    fresh = span_scores(BLOCKS[1])
    for number in range(1, len(BLOCKS)):
        with jax.named_scope(f"C_block{number}"):
            following = None
            if number + 1 < len(BLOCKS):
                held.append(cache_scores(BLOCKS[number + 1]))
                following = span_scores(BLOCKS[number + 1])
            finish(BLOCKS[number], attend(held[number], fresh))
            fresh = following
    own = take(att.at[z, y], out_ref.at[s], loc_sem.at[0])

    await_all(nothing.at[pl.ds(0, OTHER_TILES)], sent)
    for rows, count in ((early, EARLY_TILES), (late, LATE_TILES)):
        mine = jnp.logical_and(rows, mover)
        pl.when(mine)(functools.partial(await_all, nothing.at[pl.ds(0, 3 * count + 128)], moved))
        mine = jnp.logical_and(rows, jnp.logical_not(mover))
        pl.when(mine)(functools.partial(await_all, nothing.at[pl.ds(0, count)], moved))
    own.wait()
    peers = pl.ds(0, SIDE * SIDE - 1)
    with jax.named_scope("W_out"):
        await_all(out_ref.at[peers], out_recv)


def on_device(queries, span_kv, cache, prefix_len, span_len, row_source):
    shape = queries.shape
    hbm = pl.BlockSpec(memory_space=pl.ANY)
    tile = (SIDE, SIDE, ROWS, HD)
    out = pl.pallas_call(
        kernel,
        out_shape=pltpu.VMEM((SIDE * SIDE, ROWS, HD), jnp.bfloat16),
        in_specs=[hbm] * 6,
        out_specs=pl.BlockSpec(memory_space=pltpu.VMEM),
        scratch_shapes=[
            pltpu.VMEM(tile, jnp.bfloat16),
            pltpu.VMEM((SIDE, EARLY, ROWS, HD), jnp.bfloat16),
            pltpu.VMEM(tile, jnp.bfloat16),
            pltpu.VMEM((SIDE, SIDE, ROWS, 2 * HD), jnp.bfloat16),
            pltpu.VMEM((SIDE, EARLY, ROWS, 2 * HD), jnp.bfloat16),
            pltpu.VMEM((SIDE, SIDE, ROWS, 2 * HD), jnp.bfloat16),
            pltpu.VMEM((RING * 2, SHARD, 2 * HD), jnp.bfloat16),
            pltpu.SMEM((8,), jnp.int32),
            pltpu.SMEM((8,), jnp.int32),
            pltpu.VMEM((8, TOK), jnp.int32),
            pltpu.VMEM((TOK, TOK), jnp.bfloat16),
            pltpu.VMEM((TOK, HD), jnp.bfloat16),
            pltpu.VMEM(tile, jnp.bfloat16),
            pltpu.SemaphoreType.REGULAR((SIDE,)),
            pltpu.SemaphoreType.REGULAR((SIDE,)),
            pltpu.VMEM((3 * EARLY_TILES + 128, ROWS, HD), jnp.bfloat16),
            pltpu.SemaphoreType.DMA((8,)),
            pltpu.SemaphoreType.DMA,
            pltpu.SemaphoreType.DMA,
            pltpu.SemaphoreType.DMA((2, 2)),
            pltpu.SemaphoreType.DMA((2,)),
            pltpu.SemaphoreType.DMA,
            pltpu.SemaphoreType.DMA((EARLY,)),
            pltpu.SemaphoreType.DMA((SIDE,)),
            pltpu.SemaphoreType.DMA,
            pltpu.SemaphoreType.DMA,
            pltpu.SemaphoreType.DMA((3,)),
        ],
        compiler_params=pltpu.CompilerParams(collective_id=0, has_side_effects=True),
    )(
        queries.reshape(tile),
        span_kv,
        cache,
        prefix_len,
        span_len,
        row_source,
    )
    return out.reshape(shape)


def solution(mesh):
    in_specs = (
        P(None, None, "seq", "tp", None),
        P(None, None, "seq", None),
        P("seq", "tp", None),
        P(),
        P(),
        P(),
    )
    out_specs = P(None, None, "seq", "tp", None)
    return jax.shard_map(on_device, mesh=mesh, in_specs=in_specs, out_specs=out_specs, check_vma=False)
```

```python
import functools
import math

import jax
import jax.numpy as jnp
from jax import lax
from jax.experimental import pallas as pl
from jax.experimental.pallas import tpu as pltpu
from jax.sharding import PartitionSpec as P

MESH = pl.DeviceIdType.MESH
SIDE = 8
RING = 4
ROWS = 8
HD = 128
TOK = 512
SHARD = 256
EARLY = 4
EARLY_TILES = 3 * 8 + 3 * 7 * 4 + 4 * 8
LATE_TILES = 7 * 8 + 7 * 4
OTHER_TILES = 7 * 64 + 63
GROUP = 64
FAR_FIRST = (4, 3, 5, 2, 6, 1, 7)
BLOCKS = ((0, 2), (2, 4), (4, 6), (6, 8))
Y_ORDER = (0, 1, 2, 3, 4, 5, 6, 7)


def kernel(
    q_hbm,
    kv_hbm,
    cache_hbm,
    plen_hbm,
    slen_hbm,
    rs_hbm,
    out_ref,
    q_mid,
    q_up,
    q_all,
    kv_mid,
    kv_up,
    kv_all,
    stored,
    plen,
    slen,
    rs,
    pick,
    q_tab,
    att,
    known_y,
    known_z,
    nothing,
    loc_sem,
    sent,
    moved,
    z_recv,
    up_recv,
    q_done,
    low_done,
    high_done,
    swap_recv,
    out_recv,
    ring_recv,
):
    s = lax.axis_index("seq")
    t = lax.axis_index("tp")
    y, z = s // SIDE, s % SIDE
    x, core = t // 2, t % 2
    other = x * 2 + 1 - core
    x_right, x_left, x_far = lax.rem(x + 1, RING), lax.rem(x + RING - 1, RING), lax.rem(x + 2, RING)
    right, left, far = x_right * 2 + core, x_left * 2 + core, x_far * 2 + core
    ys = [lax.rem(y + d, SIDE) for d in range(SIDE)]

    rank = y

    def signal(semaphore, **where):
        pl.semaphore_signal(semaphore, inc=1, device_id=where, device_id_type=MESH)

    barrier = pltpu.get_barrier_semaphore()
    for peer in (other, right, left):
        signal(barrier, tp=peer)
    for step in range(1, SIDE):
        pl.when(step > z)(functools.partial(signal, barrier, seq=y * SIDE + step))
        pl.when(step > rank)(functools.partial(signal, barrier, seq=Y_ORDER[step] * SIDE + z))
    with jax.named_scope("W_barrier"):
        pl.semaphore_wait(barrier, z + rank + 3)
    for step in range(SIDE - 1):
        pl.when(step < z)(functools.partial(signal, known_z.at[z], seq=y * SIDE + step))
        pl.when(step < rank)(functools.partial(signal, known_y.at[rank], seq=Y_ORDER[step] * SIDE + z))

    def push(src, dst, send, recv, **where):
        copy = pltpu.make_async_remote_copy(
            src_ref=src, dst_ref=dst, send_sem=send, recv_sem=recv, device_id=where, device_id_type=MESH
        )
        copy.start()
        return copy

    def take(src, dst, sem):
        copy = pltpu.make_async_copy(src, dst, sem)
        copy.start()
        return copy

    def await_all(ref, sem):
        pltpu.make_async_copy(ref, ref, sem).wait()

    mover = core == 1
    early, late = z < EARLY, z >= EARLY
    low_z, high_z = pl.ds(0, EARLY), pl.ds(EARLY, EARLY)
    queries = (0, q_hbm, q_mid, q_up, q_all)
    span = (1, kv_hbm, kv_mid, kv_up, kv_all)

    def streams(step, *args):
        pl.when(mover)(functools.partial(step, *span, *args))
        step(*queries, *args)

    def at_z(to):
        return {"seq": y * SIDE + to}

    def at_y(to):
        return {"seq": to * SIDE + z}

    def send_z(i, src, mid, up, every, to):
        push(src.at[:, to], mid.at[z], moved, z_recv.at[i, z // EARLY], **at_z(to))

    def send_z_known(to):
        pl.semaphore_wait(known_z.at[to], 1)
        streams(send_z, to)

    def send_up(i, src, mid, up, every, to):
        push(src.at[to, high_z], up.at[y], moved, up_recv.at[i], **at_y(to))

    def send_up_known(step):
        pl.semaphore_wait(known_y.at[step], 1)
        streams(send_up, Y_ORDER[step])

    def own_start(i, src, mid, up, every):
        pltpu.make_async_copy(src.at[:, z], mid.at[z], loc_sem.at[2 * i]).start()
        pl.when(early)(pltpu.make_async_copy(src.at[y, high_z], up.at[y], loc_sem.at[2 * i + 1]).start)

    for step in reversed(range(SIDE - 1)):
        pl.when(step < z)(functools.partial(streams, send_z, step))
    for step in range(SIDE - 1):
        pl.when(jnp.logical_and(early, step < rank))(functools.partial(streams, send_up, Y_ORDER[step]))
    streams(own_start)

    shard = cache_hbm.at[0]
    push(shard, stored.at[t], sent, ring_recv.at[0], tp=right)
    push(shard, stored.at[t], sent, ring_recv.at[0], tp=left)
    push(shard, stored.at[t], sent, ring_recv.at[2], tp=other)
    own_shard = take(shard, stored.at[t], loc_sem.at[4])
    small = [
        take(plen_hbm, plen, loc_sem.at[5]),
        take(slen_hbm, slen, loc_sem.at[6]),
        take(rs_hbm, rs, loc_sem.at[7]),
    ]
    for load in small:
        load.wait()

    source = rs[pl.ds(z, 1), :].astype(jnp.float32)
    source = jnp.broadcast_to(source, (HD, TOK)).T
    row = lax.broadcasted_iota(jnp.int32, (TOK, HD), 0).astype(jnp.float32)
    lane = lax.broadcasted_iota(jnp.int32, (TOK, HD), 1).astype(jnp.float32)
    places = [
        jnp.sum(jnp.where(source == lane + float(part * HD), row, 0.0), axis=0, keepdims=True)
        for part in range(TOK // HD)
    ]
    place = jnp.concatenate(places, axis=1)
    source = jnp.swapaxes(source.reshape(SIDE, SIDE, ROWS, HD), 0, 1).reshape(TOK, HD)
    for part in range(TOK // HD):
        pick[:, part * HD : (part + 1) * HD] = jnp.where(source == lane + float(part * HD), 1.0, 0.0).astype(
            jnp.bfloat16
        )

    with jax.named_scope("W_upper"):
        for step in range(1, SIDE):
            pl.when(jnp.logical_and(early, step > rank))(functools.partial(send_up_known, step))
        for step in range(1, SIDE):
            open_now = step > z if step < EARLY else jnp.logical_and(late, step > z)
            pl.when(open_now)(functools.partial(send_z_known, step))
        for step in range(1, SIDE):
            pl.when(jnp.logical_and(late, step > rank))(
                functools.partial(pl.semaphore_wait, known_y.at[step], 1)
            )

    low, high = pl.ds(0, SHARD // 2), pl.ds(SHARD // 2, SHARD // 2)
    with jax.named_scope("W_ring01"):
        await_all(stored.at[pl.ds(0, 2)], ring_recv.at[0])
    push(stored.at[left, low], stored.at[left, low], sent, ring_recv.at[1], tp=right)
    push(stored.at[right, high], stored.at[right, high], sent, ring_recv.at[1], tp=left)
    push(stored.at[left], stored.at[left], sent, ring_recv.at[2], tp=other)
    push(stored.at[right], stored.at[right], sent, ring_recv.at[2], tp=other)

    def send_y(i, src, mid, up, every, part, which, semaphores):
        for d in FAR_FIRST:
            push(mid.at[part, ys[d]], every.at[y, part], moved, semaphores[i], **at_y(ys[d]))

    def own_wait(i, src, mid, up, every):
        pltpu.make_async_copy(src.at[:, z], mid.at[z], loc_sem.at[2 * i]).wait()

    def low_part(i, src, mid, up, every):
        with jax.named_scope("W_low"):
            own_wait(i, src, mid, up, every)
            await_all(mid.at[pl.ds(0, EARLY - 1)], z_recv.at[i, 0])
        send_y(i, src, mid, up, every, low_z, 0, (q_done, low_done.at[0]))
        take(mid.at[low_z, y], every.at[y, low_z], loc_sem.at[2 * i])

    def up_wait(i, src, mid, up, every):
        with jax.named_scope("W_up"):
            pltpu.make_async_copy(src.at[y, high_z], up.at[y], loc_sem.at[2 * i + 1]).wait()
            await_all(up.at[pl.ds(0, SIDE - 1)], up_recv.at[i])

    def up_part(i, src, mid, up, every, to):
        push(up.at[:, to - EARLY], every.at[:, z], moved, (q_done, low_done.at[z])[i], **at_z(to))

    def early_part():
        streams(low_part)
        streams(up_wait)
        for to in range(EARLY, SIDE):
            with jax.named_scope("W_far"):
                pl.semaphore_wait(known_z.at[to], 1)
            pl.when(mover)(functools.partial(up_part, *span, to))
        for to in range(EARLY, SIDE):
            up_part(*queries, to)

    pl.when(early)(early_part)

    def high_part(i, src, mid, up, every):
        with jax.named_scope("W_high"):
            pl.when(late)(functools.partial(own_wait, i, src, mid, up, every))
            pl.when(late)(functools.partial(await_all, mid.at[pl.ds(0, EARLY - 1)], z_recv.at[i, 1]))
            pl.when(early)(functools.partial(await_all, mid.at[pl.ds(0, EARLY)], z_recv.at[i, 1]))
        send_y(i, src, mid, up, every, high_z, 1, (q_done, high_done.at[y]))
        take(mid.at[high_z, y], every.at[y, high_z], loc_sem.at[2 * i + 1])

    streams(high_part)

    with jax.named_scope("W_ring34"):
        await_all(stored.at[0], ring_recv.at[1])
    push(stored.at[far], stored.at[far], sent, ring_recv.at[2], tp=other)

    def own_low_wait(i, src, mid, up, every):
        pltpu.make_async_copy(mid.at[low_z, y], every.at[y, low_z], loc_sem.at[2 * i]).wait()

    def own_high_wait(i, src, mid, up, every):
        pltpu.make_async_copy(mid.at[high_z, y], every.at[y, high_z], loc_sem.at[2 * i + 1]).wait()

    def hand(piece):
        push(piece, piece, moved, swap_recv, tp=other)

    def hand_low_all():
        with jax.named_scope("W_kvlow"):
            own_low_wait(*span)
            await_all(kv_all.at[pl.ds(0, SIDE - 1), low_z], low_done.at[0])
        hand(kv_all.at[:, low_z])

    def hand_low_z(step):
        piece = kv_all.at[:, step]
        with jax.named_scope("W_kvlow"):
            await_all(piece, low_done.at[step])
        hand(piece)

    def hand_high(step):
        piece = kv_all.at[step, high_z]
        with jax.named_scope("W_kv2"):
            pl.when(step == y)(functools.partial(own_high_wait, *span))
            pl.when(step != y)(functools.partial(await_all, piece, high_done.at[step]))
        hand(piece)

    def hand_over_early():
        hand_low_all()
        for step in Y_ORDER:
            hand_high(step)

    def hand_over_late():
        hand_low_z(0)
        for step in Y_ORDER[:4]:
            hand_high(step)
        hand_low_z(1)
        for step in Y_ORDER[4:]:
            hand_high(step)
        hand_low_z(2)
        hand_low_z(3)

    def hand_over():
        pl.when(early)(hand_over_early)
        pl.when(late)(hand_over_late)

    pl.when(mover)(hand_over)

    def early_queries():
        own_low_wait(*queries)
        await_all(q_all.at[pl.ds(0, SIDE - 1)], q_done)

    def late_queries():
        await_all(nothing.at[pl.ds(0, (SIDE - 1) * EARLY + SIDE * EARLY)], q_done)

    with jax.named_scope("W_q2"):
        own_high_wait(*queries)
        pl.when(early)(early_queries)
        pl.when(late)(late_queries)
    with jax.named_scope("W_ringall"):
        own_shard.wait()
        await_all(stored.at[pl.ds(0, RING)], ring_recv.at[2])

    rate = math.log2(math.e) / math.sqrt(HD)
    contract = (((1,), (1,)), ((), ()))
    keys = RING * 2 * SHARD
    limit = plen[z]
    live = slen[z]

    def cache_scores(groups):
        rows = slice(groups[0] * GROUP, groups[1] * GROUP)
        rows_q = jnp.dot(pick[rows, :], q_all[...].reshape(TOK, HD), preferred_element_type=jnp.float32)
        rows_q = rows_q.astype(jnp.bfloat16)
        q_tab[rows, :] = rows_q
        scores = lax.dot_general(
            rows_q, stored[:, :, :HD].reshape(keys, HD), contract, preferred_element_type=jnp.float32
        )
        seen = lax.broadcasted_iota(jnp.int32, scores.shape, 1) < limit
        return jnp.where(seen, scores, -jnp.inf)

    def tokens(groups, width):
        count = lax.broadcasted_iota(jnp.int32, ((groups[1] - groups[0]) * GROUP, width), 0)
        in_group = lax.bitwise_and(count, GROUP - 1)
        return (in_group - lax.bitwise_and(in_group, ROWS - 1)) * SIDE + (
            lax.bitwise_and(in_group, ROWS - 1) + ((count - in_group) // SIDE + groups[0] * ROWS)
        )

    def span_scores(groups):
        rows = q_tab[groups[0] * GROUP : groups[1] * GROUP, :]
        scores = lax.dot_general(
            rows, kv_all[:, :, :, :HD].reshape(TOK, HD), contract, preferred_element_type=jnp.float32
        )
        return jnp.where(place <= tokens(groups, TOK).astype(jnp.float32), scores, -jnp.inf)

    def send_out(to, d):
        push(att.at[to, ys[d]], out_ref.at[s], sent, out_recv, seq=ys[d] * SIDE + to)

    def cache_part(held):
        top = jnp.max(held, axis=1, keepdims=True)
        held = jnp.exp2((held - top) * rate).astype(jnp.bfloat16)
        values = jnp.concatenate([stored[:, :, HD:].reshape(keys, HD), jnp.ones((keys, HD), jnp.bfloat16)], axis=1)
        return top, jnp.dot(held, values, preferred_element_type=jnp.float32)

    def span_part(fresh, top):
        fresh = jnp.exp2((fresh - top) * rate).astype(jnp.bfloat16)
        values = jnp.concatenate([kv_all[:, :, :, HD:].reshape(TOK, HD), jnp.ones((TOK, HD), jnp.bfloat16)], axis=1)
        return jnp.dot(fresh, values, preferred_element_type=jnp.float32)

    def attend(held, fresh):
        top = jnp.maximum(jnp.max(held, axis=1, keepdims=True), jnp.max(fresh, axis=1, keepdims=True))
        held = jnp.exp2((held - top) * rate).astype(jnp.bfloat16)
        values = jnp.concatenate([stored[:, :, HD:].reshape(keys, HD), jnp.ones((keys, HD), jnp.bfloat16)], axis=1)
        return jnp.dot(held, values, preferred_element_type=jnp.float32) + span_part(fresh, top)

    def attend_late(before, total, fresh):
        top = jnp.maximum(before, jnp.max(fresh, axis=1, keepdims=True))
        return total * jnp.exp2((before - top) * rate) + span_part(fresh, top)

    def finish(groups, total):
        result = total[:, :HD] / total[:, HD:]
        result = jnp.where(tokens(groups, HD) < live, result, 0.0).astype(jnp.bfloat16)
        att[groups[0] : groups[1]] = result.reshape(groups[1] - groups[0], SIDE, ROWS, HD)
        for to in range(*groups):
            for d in FAR_FIRST:
                send_out(to, d)
            pl.when(to != z)(functools.partial(send_out, to, 0))

    with jax.named_scope("C_cache0"):
        top, total = cache_part(cache_scores(BLOCKS[0]))
        held = [None, cache_scores(BLOCKS[1])]
    with jax.named_scope("W_swap"):
        pl.when(jnp.logical_not(mover))(functools.partial(await_all, kv_all, swap_recv))
    with jax.named_scope("C_block0"):
        finish(BLOCKS[0], attend_late(top, total, span_scores(BLOCKS[0])))
    fresh = span_scores(BLOCKS[1])
    for number in range(1, len(BLOCKS)):
        with jax.named_scope(f"C_block{number}"):
            following = None
            if number + 1 < len(BLOCKS):
                held.append(cache_scores(BLOCKS[number + 1]))
                following = span_scores(BLOCKS[number + 1])
            finish(BLOCKS[number], attend(held[number], fresh))
            fresh = following
    own = take(att.at[z, y], out_ref.at[s], loc_sem.at[0])

    await_all(nothing.at[pl.ds(0, OTHER_TILES)], sent)
    for rows, count in ((early, EARLY_TILES), (late, LATE_TILES)):
        mine = jnp.logical_and(rows, mover)
        pl.when(mine)(functools.partial(await_all, nothing.at[pl.ds(0, 3 * count + 128)], moved))
        mine = jnp.logical_and(rows, jnp.logical_not(mover))
        pl.when(mine)(functools.partial(await_all, nothing.at[pl.ds(0, count)], moved))
    own.wait()
    peers = pl.ds(0, SIDE * SIDE - 1)
    with jax.named_scope("W_out"):
        await_all(out_ref.at[peers], out_recv)


def on_device(queries, span_kv, cache, prefix_len, span_len, row_source):
    shape = queries.shape
    hbm = pl.BlockSpec(memory_space=pl.ANY)
    tile = (SIDE, SIDE, ROWS, HD)
    out = pl.pallas_call(
        kernel,
        out_shape=pltpu.VMEM((SIDE * SIDE, ROWS, HD), jnp.bfloat16),
        in_specs=[hbm] * 6,
        out_specs=pl.BlockSpec(memory_space=pltpu.VMEM),
        scratch_shapes=[
            pltpu.VMEM(tile, jnp.bfloat16),
            pltpu.VMEM((SIDE, EARLY, ROWS, HD), jnp.bfloat16),
            pltpu.VMEM(tile, jnp.bfloat16),
            pltpu.VMEM((SIDE, SIDE, ROWS, 2 * HD), jnp.bfloat16),
            pltpu.VMEM((SIDE, EARLY, ROWS, 2 * HD), jnp.bfloat16),
            pltpu.VMEM((SIDE, SIDE, ROWS, 2 * HD), jnp.bfloat16),
            pltpu.VMEM((RING * 2, SHARD, 2 * HD), jnp.bfloat16),
            pltpu.SMEM((8,), jnp.int32),
            pltpu.SMEM((8,), jnp.int32),
            pltpu.VMEM((8, TOK), jnp.int32),
            pltpu.VMEM((TOK, TOK), jnp.bfloat16),
            pltpu.VMEM((TOK, HD), jnp.bfloat16),
            pltpu.VMEM(tile, jnp.bfloat16),
            pltpu.SemaphoreType.REGULAR((SIDE,)),
            pltpu.SemaphoreType.REGULAR((SIDE,)),
            pltpu.VMEM((3 * EARLY_TILES + 128, ROWS, HD), jnp.bfloat16),
            pltpu.SemaphoreType.DMA((8,)),
            pltpu.SemaphoreType.DMA,
            pltpu.SemaphoreType.DMA,
            pltpu.SemaphoreType.DMA((2, 2)),
            pltpu.SemaphoreType.DMA((2,)),
            pltpu.SemaphoreType.DMA,
            pltpu.SemaphoreType.DMA((EARLY,)),
            pltpu.SemaphoreType.DMA((SIDE,)),
            pltpu.SemaphoreType.DMA,
            pltpu.SemaphoreType.DMA,
            pltpu.SemaphoreType.DMA((3,)),
        ],
        compiler_params=pltpu.CompilerParams(collective_id=0, has_side_effects=True),
    )(
        queries.reshape(tile),
        span_kv,
        cache,
        prefix_len,
        span_len,
        row_source,
    )
    return out.reshape(shape)


def solution(mesh):
    in_specs = (
        P(None, None, "seq", "tp", None),
        P(None, None, "seq", None),
        P("seq", "tp", None),
        P(),
        P(),
        P(),
    )
    out_specs = P(None, None, "seq", "tp", None)
    return jax.shard_map(on_device, mesh=mesh, in_specs=in_specs, out_specs=out_specs, check_vma=False)
```
